32 devices in a mesh: row: 8 (over y, x, core), col: 4 (over z).
Axes of the slice: x: 2, y: 2, z: 4, core: 2. Of those that a mesh axis runs over, the one named last changes fastest.
Arguments:
- struct_basis: float32 [8192, 1024], P(('row', 'col')), may hold values from -6 to 6
- fluid_basis: float32 [4096, 1024], P(('row', 'col')), may hold values from -6 to 6
- stiff_tiles: float32 [64, 4, 128, 128], P(('row', 'col')), may hold values from -0.0029296875 to 0.0029296875
- mass_tiles: float32 [64, 4, 128, 128], P(('row', 'col')), may hold values from -0.0029296875 to 0.0029296875
- fluid_stiff_tiles: float32 [32, 4, 128, 128], P(('row', 'col')), may hold values from -0.00390625 to 0.00390625
- fluid_mass_tiles: float32 [32, 4, 128, 128], P(('row', 'col')), may hold values from -0.00390625 to 0.00390625
- struct_cols: int32 [64, 4], P(('row', 'col')), may hold values from 0 to 3
- fluid_cols: int32 [32, 4], P(('row', 'col')), may hold values from 0 to 2
- wet_rows: int32 [1024], P(('row', 'col')), may hold values from 0 to 127
- wet_dest: int32 [1024, 1], P(('row', 'col')), may hold values from 0 to 31; in each aligned block of 32 rows (0 to 31, 32 to 63, ...) at most 2 rows name the same one
- coupling: float32 [8192, 64], P(('row', 'col')), may hold values from -0.0078125 to 0.0078125
Outputs:
- stiff_red: float32 [1024, 1024], P('row', 'col')
- mass_red: float32 [1024, 1024], P('row', 'col')
- fluid_stiff_red: float32 [1024, 1024], P('row', 'col')
- fluid_mass_red: float32 [1024, 1024], P('row', 'col')
- coupling_red: float32 [1024, 1024], P('row', 'col')
The draws below stay inside these ranges and needn't reach their ends.
Inputs may be any that keep to these rules, and one draw needn't show every extreme that they name: `wet_dest`: among the 32 entries of one block, no block number is named more than 2 times, and some block number is named exactly 2 times in every draw.
All inputs are finite; a program needn't handle non-finite values.
Results may differ from the reference program's by a relative error of at most 0.0003.
Values sent between devices are 32-bit elements; how exact they have to be, the bound alone decides.
A program may use at most 128 MiB of HBM per device.

```python
import math
import jax
import jax.numpy as jnp
import numpy as np
from jax import lax

R = 1024
TILE = 128
NB = 4
HALO = 1
CAP = 2
STILE_DEV = 2
ATILE_DEV = 1
SHARDS = 32
WET_DEV = 32
AROWS_DEV = 128
NS = 8192
NA = 4096
NREC = 64
N_ROW = 8
N_COL = 4


def with_ends(values, key, low, largest):
    place = [jax.random.randint(jax.random.fold_in(key, axis), (), 0, length) for axis, length in enumerate(values.shape)]
    widest = values.shape.index(max(values.shape))
    neighbour = place[:widest] + [(place[widest] + 1) % values.shape[widest]] + place[widest + 1:]
    return values.at[tuple(place)].set(low).at[tuple(neighbour)].set(largest)


def with_spikes(entries, stream_key, source, target, blocks, factor):
    owner, partner = [(jnp.arange(entries.shape[axis_at]) // (entries.shape[axis_at] // blocks)).reshape([-1 if axis == axis_at else 1 for axis in range(entries.ndim)]) for axis_at in (source, target)]
    chosen = jax.random.permutation(stream_key, blocks)[partner]
    strong = (owner == chosen) | (owner == (partner + blocks // 2) % blocks)
    return jnp.where(strong, factor * entries, entries)


def block_levels(own_key, shape, cuts, least, high):
    level, own = 1.0, jax.random.fold_in(own_key, 6)
    for position, blocks in cuts:
        draws = jnp.exp(jax.random.uniform(jax.random.fold_in(own, position), (blocks,), jnp.float32, least / len(cuts), high / len(cuts)))
        level = level * jnp.repeat(draws, shape[position] // blocks).reshape([-1 if axis == position else 1 for axis in range(len(shape))])
    return level


def assign_block(stream_key, own, number, rows, count, top, bound, lean):
    order = jax.random.permutation(stream_key, count)
    packed, common = load_shares(count, rows * top, bound, lean, True), load_shares(count, rows * top, bound, lean, False)
    places = jnp.arange(count)

    def named(lengths, rotation):
        used = int((lengths > 0).sum())
        fixed = max(1, used // 4)
        moved = fixed + (places - fixed + rotation * (used - fixed)) % max(1, count - fixed)
        return jnp.zeros((count,), jnp.int32).at[order[jnp.where(places < fixed, places, moved)]].set(jnp.asarray(lengths, jnp.int32))

    lengths = jnp.where(number % 4 == 0, named(packed, number // 4), named(common, number - number // 4 - 1))
    mixed = jax.random.permutation(jax.random.fold_in(own, 3), count)
    donor, receiver = mixed[0:count // 2 * 2:2], mixed[1:count // 2 * 2:2]
    margin = jnp.minimum(lengths[donor] - 1, bound - lengths[receiver]) // 2
    margin = jnp.where((donor == order[0]) | (receiver == order[0]) | (lengths[receiver] == 0), 0, jnp.maximum(margin, 0))
    moved = jax.random.randint(jax.random.fold_in(own, 4), (count // 2,), 0, 1 << 20) % (margin + 1)
    lengths = lengths.at[donor].add(-moved).at[receiver].add(moved)
    labels = jnp.searchsorted(jnp.cumsum(lengths), jnp.arange(rows * top), side="right").astype(jnp.int32)
    table = labels.reshape(top, rows).T
    table = table[jax.random.permutation(jax.random.fold_in(own, 1), rows)]
    rotation = jax.random.randint(jax.random.fold_in(own, 2), (rows, 1), 0, top)
    return jnp.take_along_axis(table, (jnp.arange(top)[None, :] + rotation) % top, axis=1)


def load_shares(amount, total, limit, skew, full):
    loads = [(1 << 20) // math.isqrt(standing ** skew) + 1 for standing in range(1, amount + 1)]
    largest = limit if full else min(limit, max(-(-total // amount), total * loads[0] // sum(loads)))
    least = 1 if total - largest >= amount - 1 else 0
    given, rest = [largest] + [least] * (amount - 1), total - largest - least * (amount - 1)
    while rest > 0:
        candidates = [i for i in range(1, amount) if given[i] < largest] or [i for i in range(1, amount) if given[i] < limit]
        pool, budget = sum([loads[i] for i in candidates]), rest
        for i in candidates:
            extra = min(limit - given[i], max(1, budget * loads[i] // pool), rest)
            given[i] = given[i] + extra
            rest = rest - extra
    return np.array(given)


def noise(key, shape, deviation, most, shards=(), kind=jnp.bfloat16):
    values = jax.random.normal(key, shape, jnp.float32) * deviation
    if len(shards) > 0:
        values = block_levels(key, shape, shards, -0.22, 0.18) * values
    return jnp.clip(values, min=-most, max=most).astype(kind)


def noise_with(own_key, shape, scale, reach, shards, heavy, held_as=jnp.bfloat16):
    values = scale * jax.random.normal(own_key, shape, jnp.float32)
    if shards:
        values = values * block_levels(own_key, shape, shards, -0.22, 0.18)
    return jnp.clip(with_spikes(values, jax.random.fold_in(own_key, 3), *heavy), -reach, reach).astype(held_as)


def setup_inputs(seed: int = 0) -> dict:
    streams_of = jax.random.split(jax.random.key(seed), 12)
    struct_basis = noise_with(streams_of[0], (NS, R), 1.0, 6.0, ((0, 32),), (0, 1, 32, 2.75), jnp.float32)
    fluid_basis = noise_with(streams_of[1], (NA, R), 1.0, 6.0, ((0, 32),), (0, 1, 32, 2.75), jnp.float32)
    stiff_tiles = noise(streams_of[2], (STILE_DEV * SHARDS, NB, TILE, TILE), (TILE * NB * NS) ** -0.5, 0.0029296875, ((0, 32),), jnp.float32)
    mass_tiles = noise(streams_of[3], (STILE_DEV * SHARDS, NB, TILE, TILE), (TILE * NB * NS) ** -0.5, 0.0029296875, ((0, 32),), jnp.float32)
    fluid_stiff_tiles = noise(streams_of[4], (ATILE_DEV * SHARDS, NB, TILE, TILE), (TILE * NB * NA) ** -0.5, 0.00390625, ((0, 32),), jnp.float32)
    fluid_mass_tiles = noise(streams_of[5], (ATILE_DEV * SHARDS, NB, TILE, TILE), (TILE * NB * NA) ** -0.5, 0.00390625, ((0, 32),), jnp.float32)
    struct_cols = with_ends(jax.random.randint(streams_of[6], (STILE_DEV * SHARDS, NB), 0, STILE_DEV + 2 * HALO), jax.random.fold_in(streams_of[6], 1), 0, (STILE_DEV + 2 * HALO) - 1).astype(jnp.int32)
    fluid_cols = with_ends(jax.random.randint(streams_of[7], (ATILE_DEV * SHARDS, NB), 0, ATILE_DEV + 2 * HALO), jax.random.fold_in(streams_of[7], 1), 0, (ATILE_DEV + 2 * HALO) - 1).astype(jnp.int32)
    wet_rows = with_ends(jax.random.randint(streams_of[8], (WET_DEV * SHARDS,), 0, AROWS_DEV), jax.random.fold_in(streams_of[8], 1), 0, AROWS_DEV - 1).astype(jnp.int32)
    wet_dest_keys = jax.random.split(jax.random.fold_in(streams_of[9], 1), (WET_DEV * SHARDS) // WET_DEV)
    wet_dest_turns = jax.random.permutation(jax.random.fold_in(streams_of[9], 3), (WET_DEV * SHARDS) // WET_DEV)
    wet_dest = jax.vmap(lambda own, number: assign_block(jax.random.fold_in(streams_of[9], 2), own, number, WET_DEV, SHARDS, 1, CAP, 2))(wet_dest_keys, wet_dest_turns).reshape((WET_DEV * SHARDS, 1))
    coupling = noise(streams_of[10], (NS, NREC), (NS * SHARDS * CAP) ** -0.5, 0.0078125, ((0, 32),), jnp.float32)
    return dict(struct_basis=struct_basis, fluid_basis=fluid_basis, stiff_tiles=stiff_tiles, mass_tiles=mass_tiles, fluid_stiff_tiles=fluid_stiff_tiles, fluid_mass_tiles=fluid_mass_tiles, struct_cols=struct_cols, fluid_cols=fluid_cols, wet_rows=wet_rows, wet_dest=wet_dest, coupling=coupling)


exact_precision = lax.Precision.HIGHEST


def tile_product(tiles, columns, extended):
    blocks = extended.reshape(-1, TILE, R)
    picked = jnp.take(blocks, columns, axis=0)
    result = jnp.einsum("tbij,tbjr->tir", tiles, picked, precision=exact_precision)
    return result.reshape(-1, R)


def congruence(left_basis, image):
    return jnp.einsum("nr,ns->rs", left_basis, image, precision=exact_precision)


def slot_numbers(targets):
    shard_count = N_ROW * N_COL
    onehot = (targets[:, None] == jnp.arange(shard_count, dtype=jnp.int32)[None, :]).astype(jnp.int32)
    before = jnp.cumsum(onehot, axis=0) - onehot
    return jnp.sum(before * onehot, axis=1).astype(jnp.int32)


def extend(basis, device, height):
    shard_count = N_ROW * N_COL
    border = HALO * TILE
    total_rows = basis.shape[0]
    start = (device * height).astype(jnp.int32)
    own_block = lax.dynamic_slice_in_dim(basis, start, height, 0)
    lower = lax.dynamic_slice_in_dim(basis, jnp.maximum(start - border, 0).astype(jnp.int32), border, 0)
    upper = lax.dynamic_slice_in_dim(basis, jnp.minimum(start + height, total_rows - border).astype(jnp.int32), border, 0)
    lower = lower * (device > 0).astype(basis.dtype)
    upper = upper * (device < shard_count - 1).astype(basis.dtype)
    return own_block, jnp.concatenate([lower, own_block, upper], axis=0)


def reference(struct_basis, fluid_basis, stiff_tiles, mass_tiles, fluid_stiff_tiles, fluid_mass_tiles, struct_cols, fluid_cols, wet_rows, wet_dest, coupling):
    shard_count = N_ROW * N_COL
    struct_height = STILE_DEV * TILE
    fluid_height = ATILE_DEV * TILE
    slot_total = shard_count * CAP
    destination = wet_dest[:, 0].reshape(shard_count, WET_DEV)
    slot_index = lax.map(slot_numbers, destination)
    source = jnp.arange(shard_count, dtype=jnp.int32)[:, None]
    target = (source * CAP + slot_index).reshape(-1).astype(jnp.int32)
    flat_dest = destination.reshape(-1)
    global_rows = (source * fluid_height + wet_rows.reshape(shard_count, WET_DEV)).reshape(-1).astype(jnp.int32)
    wet_values = jnp.take(fluid_basis, global_rows, axis=0)

    def step(totals, device):
        def device_part(array, count):
            return lax.dynamic_slice_in_dim(array, (device * count).astype(jnp.int32), count, 0)

        own_struct, extended_struct = extend(struct_basis, device, struct_height)
        own_fluid, extended_fluid = extend(fluid_basis, device, fluid_height)
        stiff_part = congruence(own_struct, tile_product(device_part(stiff_tiles, STILE_DEV), device_part(struct_cols, STILE_DEV), extended_struct))
        mass_part = congruence(own_struct, tile_product(device_part(mass_tiles, STILE_DEV), device_part(struct_cols, STILE_DEV), extended_struct))
        fstiff_part = congruence(own_fluid, tile_product(device_part(fluid_stiff_tiles, ATILE_DEV), device_part(fluid_cols, ATILE_DEV), extended_fluid))
        fmass_part = congruence(own_fluid, tile_product(device_part(fluid_mass_tiles, ATILE_DEV), device_part(fluid_cols, ATILE_DEV), extended_fluid))
        places = jnp.where(flat_dest == device, target, slot_total).astype(jnp.int32)
        received = jnp.zeros((slot_total, R), fluid_basis.dtype).at[places].set(wet_values, mode="drop")
        projected = jnp.einsum("nr,nk->rk", own_struct, device_part(coupling, struct_height), precision=exact_precision)
        coupled_part = jnp.dot(projected, received, precision=exact_precision)
        updated = (totals[0] + stiff_part, totals[1] + mass_part, totals[2] + fstiff_part, totals[3] + fmass_part, totals[4] + coupled_part)
        return updated, None

    empty_sum = jnp.zeros((R, R), struct_basis.dtype)
    totals, unused = lax.scan(step, (empty_sum, empty_sum, empty_sum, empty_sum, empty_sum), jnp.arange(shard_count, dtype=jnp.int32))
    return (totals[0], totals[1], totals[2], totals[3], totals[4])
```

```python
import functools

import jax
import jax.numpy as jnp
from jax import lax
from jax.experimental import pallas as pl
from jax.experimental.pallas import tpu as pltpu
from jax.sharding import PartitionSpec as P

TILE = 128
CAP = 2
MATS = 4
WIDE = 256
VMEM_LIMIT = 67043328
MESH = pl.DeviceIdType.MESH
F32, BF16 = jnp.float32, jnp.bfloat16


def halves(value):
    high = value.astype(BF16)
    low = (value - high.astype(F32)).astype(BF16)
    return high, low


def bits_of(size):
    return size.bit_length() - 1


def subset_offsets(bits):
    offsets = [0]
    for bit in bits:
        offsets = [base + extra for extra in (0, 1 << bit) for base in offsets]
    return offsets


def dot(a, b):
    return jnp.dot(a, b, preferred_element_type=F32)


def dot_t(a, b):
    return lax.dot_general(a, b, (((0,), (0,)), ((), ())), preferred_element_type=F32)


class Sizes:
    def __init__(self, nr, nc, rows_s, rows_f, size, wet):
        self.nr, self.nc, self.size = nr, nc, size
        self.rows_s, self.rows_f, self.wet = rows_s, rows_f, wet
        self.shards = nr * nc
        self.bm, self.bn = size // nr, size // nc
        self.col_parts = 2 if self.bn >= 2 * TILE else 1
        self.row_parts = 2
        self.parts = self.col_parts * self.row_parts
        self.hb, self.bw = self.bm // self.row_parts, self.bn // self.col_parts
        self.chunk = nc * self.bw
        self.qw = max(self.bm, TILE)
        self.some = max(1, min(nr, WIDE // wet))
        self.row_bits, self.col_bits = bits_of(nr), bits_of(nc)
        self.stages = self.row_bits + self.col_bits
        self.total_s = rows_s + 2 * TILE
        self.total_f = rows_f + 2 * TILE

    def scratch(self):
        s = self
        chunks = s.col_parts
        buffers = {
            "acc": ((s.parts, MATS, s.nr, s.nc, s.hb, s.bw), F32),
            "acc_c": ((s.parts, s.nc, s.hb, s.bw), F32),
            "halo_s": ((2, chunks, s.nc, TILE, s.bw), F32),
            "halo_f": ((2, s.rows_f, s.size), F32),
            "ktile_out": ((2, 2, TILE, TILE), F32),
            "ktile_in": ((2, 2, TILE, TILE), F32),
            "left_s": ((s.size, 3 * s.rows_s), BF16),
            "left_f": ((2, s.size, 6 * s.rows_f), BF16),
            "dense_s": ((2, max(s.rows_s, 2 * s.rows_f), 3 * max(s.total_s, s.total_f)), BF16),
            "dense_f": ((2 * s.rows_f, 3 * s.total_f), BF16),
            "ext": ((chunks, 3 * max(s.total_s, s.total_f), s.chunk), BF16),
            "image": ((2, max(3 * s.rows_s, 6 * s.rows_f), s.chunk), BF16),
            "p_out": ((s.shards, CAP, s.size), F32),
            "p_in": ((s.shards, CAP, s.size), F32),
            "p_all": ((s.shards * CAP, WIDE), F32),
            "q_out": ((s.wet, s.size), F32),
            "q_in": ((s.nr, s.wet, s.qw), F32),
            "q_left": ((2, s.qw, s.some * s.wet), BF16),
            "w_all": ((s.nr, s.wet, s.size), F32),
        }
        for stage in range(s.stages):
            buffers["landing%d" % stage] = ((s.parts, MATS, s.shards >> (stage + 1), s.hb, s.bw), F32)
        for bit in range(s.col_bits):
            buffers["landing_c%d" % bit] = ((s.parts, s.nc >> (bit + 1), s.hb, s.bw), F32)
        sems = {
            "send_sem": (s.parts, MATS, s.stages),
            "recv_sem": (s.parts, MATS, s.stages),
            "c_send": (s.parts, s.col_bits),
            "c_recv": (s.parts, s.col_bits),
            "halo_send": (2, chunks),
            "halo_recv": (2, chunks),
            "f_send": (2, 2),
            "f_recv": (2, 2),
            "w_send": (s.nr,),
            "w_recv": (s.nr,),
            "q_send": (s.nr,),
            "q_recv": (s.nr,),
            "wet_send": (1,),
            "wet_recv": (1,),
        }
        return buffers, sems


def kernel(
    s,
    struct_cols,
    fluid_cols,
    struct,
    fluid,
    stiff_tiles,
    mass_tiles,
    fstiff_tiles,
    fmass_tiles,
    coupling_t,
    wet_rows,
    wet_dest,
    outs,
    *refs,
):
    buffers, sems = s.scratch()
    ref = dict(zip(list(buffers) + list(sems), refs, strict=True))
    nr, nc, shards, size = s.nr, s.nc, s.shards, s.size
    rows_s, rows_f = s.rows_s, s.rows_f
    bm, bn, hb, bw = s.bm, s.bn, s.hb, s.bw
    total_s, total_f = s.total_s, s.total_f
    stages = s.stages
    acc, acc_c = ref["acc"], ref["acc_c"]
    row, col = lax.axis_index("row"), lax.axis_index("col")
    block = row * nc + col
    following = lax.rem(block + 1, shards)
    previous = lax.rem(block + shards - 1, shards)
    after = (following // nc, lax.rem(following, nc))
    before = (previous // nc, lax.rem(previous, nc))
    my_row = [lax.rem(row // (1 << b), 2) for b in range(s.row_bits)]
    my_col = [lax.rem(col // (1 << b), 2) for b in range(s.col_bits)]
    row_peer = [(row + (1 - 2 * my_row[b]) * (1 << b), col) for b in range(s.row_bits)]
    col_peer = [(row, col + (1 - 2 * my_col[b]) * (1 << b)) for b in range(s.col_bits)]
    has_next, has_prev = block < shards - 1, block > 0

    def flipped(mask):
        return row + sum(((1 - 2 * my_row[b]) * (1 << b) for b in range(s.row_bits) if mask >> b & 1), 0)

    def ahead(where):
        r, c = where // nc, lax.rem(where, nc)
        even = lax.rem(r, 2) == 0
        turning = (c == nc - 1) | (c == nc // 2 - 1)
        return (turning & even) | (jnp.logical_not(turning) & (c >= nc // 2))

    give_next = has_next & ahead(block)
    take_next = has_next & jnp.logical_not(ahead(block))
    take_prev = has_prev & ahead(previous)
    give_prev = has_prev & jnp.logical_not(ahead(previous))

    barrier = pltpu.get_barrier_semaphore()

    def device_at(distance):
        other = lax.rem(block + distance, shards)
        return other, (other // nc, lax.rem(other, nc))

    def greet(distance, carry):
        pl.semaphore_signal(barrier, inc=1, device_id=device_at(distance)[1], device_id_type=MESH)
        return carry

    lax.fori_loop(1, shards, greet, 0)

    def remote(source, target, send, recv, device):
        return pltpu.make_async_remote_copy(
            src_ref=source, dst_ref=target, send_sem=send, recv_sem=recv, device_id=device, device_id_type=MESH
        )

    def wide(q):
        return pl.ds(pl.multiple_of(q * WIDE, WIDE), WIDE)

    def halo_pieces(side, ch):
        start, device = ((rows_s - TILE, after), (0, before))[side]
        return [
            remote(
                struct.at[pl.ds(start, TILE), pl.ds(c * bn + ch * bw, bw)],
                ref["halo_s"].at[side, ch, c],
                ref["halo_send"].at[side, ch],
                ref["halo_recv"].at[side, ch],
                device,
            )
            for c in range(nc)
        ]

    def halo_whole(side, ch):
        here = ref["halo_s"].at[side, ch]
        return remote(here, here, ref["halo_send"].at[side, ch], ref["halo_recv"].at[side, ch], (after, before)[side])

    def start_halos(ch):
        for side, sends in ((0, has_next), (1, has_prev)):

            @pl.when(sends)
            def _(side=side):
                for piece in halo_pieces(side, ch):
                    piece.start()

    def fluid_copies(side):
        device = (after, before)[side]
        pairs = [(fluid, ref["halo_f"].at[side]), (ref["ktile_out"].at[side], ref["ktile_in"].at[side])]
        return [
            remote(source, target, ref["f_send"].at[side, k], ref["f_recv"].at[side, k], device)
            for k, (source, target) in enumerate(pairs)
        ]

    def start_fluid():
        for side, sends in ((0, give_next), (1, give_prev)):

            @pl.when(sends)
            def _(side=side):
                for piece in fluid_copies(side):
                    piece.start()

    def send_wet(distance, carry):
        other, device = device_at(distance)
        remote(
            ref["p_out"].at[other], ref["p_in"].at[block], ref["wet_send"].at[0], ref["wet_recv"].at[0], device
        ).start()
        return carry

    wet_all = remote(
        ref["p_out"].at[pl.ds(0, shards - 1)],
        ref["p_in"].at[pl.ds(0, shards - 1)],
        ref["wet_send"].at[0],
        ref["wet_recv"].at[0],
        after,
    )

    far = [mask for mask in range(2, nr, 2)]

    def w_copy(mask, near):
        slot = flipped(mask) if near else row
        device = (flipped(1), col) if near else (flipped(mask), col)
        place = mask + 1 if near else mask
        return remote(
            ref["w_all"].at[slot], ref["w_all"].at[slot], ref["w_send"].at[place], ref["w_recv"].at[place], device
        )

    def q_copy(mask):
        peer = flipped(mask)
        start = pl.multiple_of(peer * bm // s.qw * s.qw, s.qw)
        return remote(
            ref["q_out"].at[:, pl.ds(start, s.qw)],
            ref["q_in"].at[row],
            ref["q_send"].at[mask],
            ref["q_recv"].at[mask],
            (peer, col),
        )

    def order_of(part, mat):
        rows = [("row", b) for b in range(s.row_bits)]
        cols = [("col", b) for b in range(s.col_bits)]
        if part % 2:
            rows = rows[:1] + rows[1:][::-1]
        return rows + cols

    def exchange(order, stage):
        axis, bit = order[stage]
        mine = {"row": my_row, "col": my_col}
        places = {}
        for name in ("row", "col"):
            fixed = sum((mine[name][b] * (1 << b) for at, b in order[:stage] if at == name), 0)
            rest = subset_offsets(sorted(b for at, b in order[stage + 1 :] if at == name))
            places[name] = [fixed + extra for extra in rest]
        sent, kept = dict(places), dict(places)
        sent[axis] = [index + (1 - mine[axis][bit]) * (1 << bit) for index in places[axis]]
        kept[axis] = [index + mine[axis][bit] * (1 << bit) for index in places[axis]]
        peer = (row_peer if axis == "row" else col_peer)[bit]
        return sent, kept, peer

    def whole_stage(part, mat, stage):
        peer = exchange(order_of(part, mat), stage)[2]
        here = ref["landing%d" % stage].at[part, mat]
        return remote(here, here, ref["send_sem"].at[part, mat, stage], ref["recv_sem"].at[part, mat, stage], peer)

    def send(part, mat, stage):
        sent, kept, peer = exchange(order_of(part, mat), stage)
        landing = ref["landing%d" % stage]
        width = len(sent["col"])
        for place, r in enumerate(sent["row"]):
            if width == nc:
                pairs = [(acc.at[part, mat, r], landing.at[part, mat, pl.ds(place * nc, nc)])]
            else:
                pairs = [
                    (acc.at[part, mat, r, c], landing.at[part, mat, place * width + at])
                    for at, c in enumerate(sent["col"])
                ]
            for source, target in pairs:
                remote(
                    source, target, ref["send_sem"].at[part, mat, stage], ref["recv_sem"].at[part, mat, stage], peer
                ).start()

    def write_out(mat, part, total):
        ch, rh = part // s.row_parts, part % s.row_parts
        outs[mat, pl.ds(rh * hb, hb), pl.ds(ch * bw, bw)] = total

    def absorb(part, mat, stage):
        sent, kept, peer = exchange(order_of(part, mat), stage)
        landing = ref["landing%d" % stage]
        whole_stage(part, mat, stage).wait_recv()
        width = len(kept["col"])
        for place, r in enumerate(kept["row"]):
            if width == nc:

                def add(c, carry, place=place, r=r):
                    acc[part, mat, r, c] = acc[part, mat, r, c] + landing[part, mat, place * nc + c]
                    return carry

                lax.fori_loop(0, nc, add, 0)
            else:
                for at, c in enumerate(kept["col"]):
                    total = acc[part, mat, r, c] + landing[part, mat, place * width + at]
                    if stage < stages - 1:
                        acc[part, mat, r, c] = total
                    else:
                        write_out(mat, part, total)
        if stage < stages - 1:
            send(part, mat, stage + 1)

    col_order = [("col", b) for b in range(s.col_bits)]

    def c_whole(part, bit):
        here = ref["landing_c%d" % bit].at[part]
        return remote(here, here, ref["c_send"].at[part, bit], ref["c_recv"].at[part, bit], col_peer[bit])

    def c_send(part, bit):
        sent, kept, peer = exchange(col_order, bit)
        for at, c in enumerate(sent["col"]):
            remote(
                acc_c.at[part, c],
                ref["landing_c%d" % bit].at[part, at],
                ref["c_send"].at[part, bit],
                ref["c_recv"].at[part, bit],
                peer,
            ).start()

    def c_absorb(part, bit):
        sent, kept, peer = exchange(col_order, bit)
        c_whole(part, bit).wait_recv()
        for at, c in enumerate(kept["col"]):
            total = acc_c[part, c] + ref["landing_c%d" % bit][part, at]
            if bit < s.col_bits - 1:
                acc_c[part, c] = total
            else:
                write_out(MATS, part, total)
        if bit < s.col_bits - 1:
            c_send(part, bit + 1)

    def select_wet():
        places = lax.broadcasted_iota(jnp.int32, (rows_f, s.wet), 0)
        chooser = (places == wet_rows[...]).astype(F32).astype(BF16)
        high, low = halves(fluid[...])
        ref["w_all"][row] = dot_t(chooser, high) + dot_t(chooser, low)

    def project_coupling():
        ch_, cl_ = halves(coupling_t[...])
        for q in range(size // WIDE):
            at = pl.ds(q * WIDE, WIDE)
            sh, sl = halves(struct[:, at])
            value = dot(ch_, sh) + dot(ch_, sl) + dot(cl_, sh)
            for shard in range(shards):
                ref["p_out"][shard, :, at] = value[shard * CAP : (shard + 1) * CAP]

    def gather_coupling():
        dest = wet_dest[...]
        mine = (lax.broadcasted_iota(jnp.int32, (shards, s.wet), 0) == dest).astype(F32)
        below = lax.broadcasted_iota(jnp.int32, (s.wet, s.wet), 0) < lax.broadcasted_iota(
            jnp.int32, (s.wet, s.wet), 1
        )
        earlier = dot(mine.astype(BF16), below.astype(F32).astype(BF16))
        slot = jnp.sum(earlier * mine, axis=0, keepdims=True)
        target = dest.astype(F32) * CAP + slot
        places = lax.broadcasted_iota(jnp.int32, (shards * CAP, s.wet), 0).astype(F32)
        chooser = (places == target).astype(F32).astype(BF16)
        wet_all.wait_recv()
        for q in range(size // WIDE):
            at = pl.ds(q * WIDE, WIDE)
            for shard in range(shards):
                ref["p_all"][pl.ds(shard * CAP, CAP), :] = ref["p_in"][shard, :, at]
            high, low = halves(ref["p_all"][...])
            ref["q_out"][:, at] = dot_t(chooser, high) + dot_t(chooser, low)
        for mask in range(1, nr):
            q_copy(mask).start()
        own = pl.multiple_of(row * bm // s.qw * s.qw, s.qw)
        ref["q_in"][row] = ref["q_out"][:, pl.ds(own, s.qw)]

    def couple():
        for mask in range(1, nr):
            q_copy(mask).wait_recv()
        for mask in [0] + far:
            w_copy(mask, True).wait_recv()
        some, rank = s.some, s.some * s.wet
        first = pl.multiple_of(lax.rem(row * bm, s.qw), bm)
        per = WIDE // bw
        for group in range(nr // some):
            here = pl.ds(group * some, some)
            high, low = halves(ref["q_in"][here].reshape(rank, s.qw).T)
            ref["q_left"][0] = high
            ref["q_left"][1] = low
            lh, ll = ref["q_left"][0, pl.ds(first, bm)], ref["q_left"][1, pl.ds(first, bm)]
            for q in range(size // WIDE):
                wh, wl = halves(ref["w_all"][here, :, pl.ds(q * WIDE, WIDE)].reshape(rank, WIDE))
                value = dot(lh, wh) + dot(lh, wl) + dot(ll, wh)
                for k in range(per):
                    c, ch = (q * per + k) // s.col_parts, (q * per + k) % s.col_parts
                    for rh in range(s.row_parts):
                        place = ch * s.row_parts + rh, c
                        piece = value[rh * hb : (rh + 1) * hb, k * bw : (k + 1) * bw]
                        acc_c[place] = piece if group == 0 else acc_c[place] + piece
        for part in range(s.parts):
            c_send(part, 0)

    def transpose_struct():
        left = ref["left_s"]

        def step(k, carry):
            at = pl.ds(pl.multiple_of(k * TILE, TILE), TILE)
            high, low = halves(struct[:, at].T)
            left[at, pl.ds(0, rows_s)] = high
            left[at, pl.ds(rows_s, rows_s)] = high
            left[at, pl.ds(2 * rows_s, rows_s)] = low
            return carry

        lax.fori_loop(0, size // TILE, step, 0)

    def place_left_f(mats, at, first, value):
        high, low = halves(value)
        for mat in mats:
            left = ref["left_f"].at[mat]
            left[at, pl.ds(first, rows_f)] = high
            left[at, pl.ds(2 * rows_f + first, rows_f)] = high
            left[at, pl.ds(4 * rows_f + first, rows_f)] = low

    def transpose_fluid():
        def step(k, carry):
            at = pl.ds(pl.multiple_of(k * TILE, TILE), TILE)
            place_left_f((0, 1), at, 0, fluid[:, at].T)
            return carry

        lax.fori_loop(0, size // TILE, step, 0)

    def place_rows(ext, total, start, at, value):
        count = value.shape[0]
        high, low = halves(value)
        ext[pl.ds(start, count), at] = high
        ext[pl.ds(total + start, count), at] = low
        ext[pl.ds(2 * total + start, count), at] = high

    def place_own(ext, own, total, start):
        for ch in range(s.col_parts):
            for c in range(nc):
                place_rows(ext.at[ch], total, start, pl.ds(c * bw, bw), own[:, pl.ds(c * bn + ch * bw, bw)])

    def tile_sum(tiles, cols, i, c):
        tile = jnp.zeros((TILE, TILE), F32)
        for k in range(tiles.shape[1]):
            tile += jnp.where(cols[i, k] == c, tiles[i, k], 0.0)
        return tile

    def place_tile(dense, at, start, total, tile):
        high, low = halves(tile)
        dense[at, pl.ds(start, TILE)] = high
        dense[at, pl.ds(total + start, TILE)] = high
        dense[at, pl.ds(2 * total + start, TILE)] = low

    def dense_struct(tiles, mat):
        for i in range(rows_s // TILE):
            for c in range(total_s // TILE):
                place_tile(
                    ref["dense_s"].at[mat], pl.ds(i * TILE, TILE), c * TILE, total_s, tile_sum(tiles, struct_cols, i, c)
                )

    def dense_fluid(tiles, mat):
        for c in range(3):
            tile = tile_sum(tiles, fluid_cols, 0, c)
            place_tile(ref["dense_f"], pl.ds(mat * rows_f, TILE), c * TILE, total_f, tile)
            if c == 0:
                ref["ktile_out"][1, mat] = tile
            if c == 2:
                ref["ktile_out"][0, mat] = tile

    def fill_halos(ch):
        for side, comes in ((0, has_prev), (1, has_next)):

            @pl.when(comes)
            def _(side=side):
                halo_whole(side, ch).wait_recv()

            @pl.when(jnp.logical_not(comes))
            def _(side=side):
                ref["halo_s"][side, ch] = jnp.zeros((nc, TILE, bw), F32)

            start = (0, total_s - TILE)[side]
            for c in range(nc):
                place_rows(ref["ext"].at[ch], total_s, start, pl.ds(c * bw, bw), ref["halo_s"][side, ch, c])

    def fill_fluid():
        for side, comes in ((0, take_prev), (1, take_next)):

            @pl.when(comes)
            def _(side=side):
                for piece in fluid_copies(side):
                    piece.wait_recv()

            @pl.when(jnp.logical_not(comes))
            def _(side=side):
                ref["halo_f"][side] = jnp.zeros((rows_f, size), F32)
                ref["ktile_in"][side] = jnp.zeros((2, TILE, TILE), F32)

            start = (0, total_f - TILE)[side]
            for ch in range(s.col_parts):
                for c in range(nc):
                    place_rows(
                        ref["ext"].at[ch],
                        total_f,
                        start,
                        pl.ds(c * bw, bw),
                        ref["halo_f"][side, :, pl.ds(c * bn + ch * bw, bw)],
                    )
            for mat in range(2):
                place_tile(ref["dense_s"].at[0], pl.ds(mat * rows_f, TILE), start, total_f, ref["ktile_in"][side, mat].T)
        for mat in range(2):
            place_tile(ref["dense_s"].at[0], pl.ds(mat * rows_f, TILE), TILE, total_f, jnp.zeros((TILE, TILE), F32))
        per = WIDE // bw
        for ch in range(s.col_parts):

            def step(q, carry, ch=ch):
                value = dot(ref["dense_s"][0, pl.ds(0, 2 * rows_f), pl.ds(0, 3 * total_f)], ref["ext"][ch, pl.ds(0, 3 * total_f), wide(q)])
                for k in range(per):
                    at = pl.ds(pl.multiple_of((q * per + k) * bn + ch * bw, bw), bw)
                    for mat in range(2):
                        piece = value[mat * rows_f : (mat + 1) * rows_f, k * bw : (k + 1) * bw]
                        place_left_f((mat,), at, rows_f, piece.T)
                return carry

            lax.fori_loop(0, s.chunk // WIDE, step, 0)

    def image_struct(ch, mat):
        image = ref["image"].at[0]

        def step(q, carry):
            at = wide(q)
            high, low = halves(dot(ref["dense_s"][mat, pl.ds(0, rows_s), pl.ds(0, 3 * total_s)], ref["ext"][ch, pl.ds(0, 3 * total_s), at]))
            image[pl.ds(0, rows_s), at] = high
            image[pl.ds(rows_s, rows_s), at] = low
            image[pl.ds(2 * rows_s, rows_s), at] = high
            return carry

        lax.fori_loop(0, s.chunk // WIDE, step, 0)

    def image_fluid(ch):
        def step(q, carry):
            at = wide(q)
            high, low = halves(dot(ref["dense_f"][...], ref["ext"][ch, pl.ds(0, 3 * total_f), at]))
            own = [ref["ext"][ch, pl.ds(third * total_f + TILE, rows_f), at] for third in range(2)]
            for mat in range(2):
                image = ref["image"].at[mat]
                here = slice(mat * rows_f, (mat + 1) * rows_f)
                for third, (value, mine) in enumerate(((high, own[0]), (low, own[1]), (high, own[0]))):
                    image[pl.ds(2 * third * rows_f, rows_f), at] = value[here]
                    image[pl.ds((2 * third + 1) * rows_f, rows_f), at] = mine
            return carry

        lax.fori_loop(0, s.chunk // WIDE, step, 0)

    def project(left, image, ch, mat):
        per = WIDE // bw

        def step(q, carry):
            value = dot(left[...], image[pl.ds(0, left.shape[1]), wide(q)])
            for r in range(nr):
                for rh in range(s.row_parts):
                    start = r * bm + rh * hb
                    for k in range(per):
                        acc[ch * s.row_parts + rh, mat, r, q * per + k] = value[
                            start : start + hb, k * bw : (k + 1) * bw
                        ]
            return carry

        lax.fori_loop(0, s.chunk // WIDE, step, 0)
        for rh in range(s.row_parts):
            send(ch * s.row_parts + rh, mat, 0)

    select_wet()
    project_coupling()
    pl.semaphore_wait(barrier, shards - 1)
    start_halos(0)
    lax.fori_loop(1, shards, send_wet, 0)
    for mask in far:
        w_copy(mask, False).start()
    w_copy(0, True).start()
    ref["p_in"][block] = ref["p_out"][block]
    dense_struct(stiff_tiles, 0)
    dense_struct(mass_tiles, 1)
    transpose_struct()
    place_own(ref["ext"], struct, total_s, TILE)
    gather_coupling()
    for mask in far:
        w_copy(mask, False).wait_recv()
        w_copy(mask, True).start()
    dense_fluid(fstiff_tiles, 0)
    dense_fluid(fmass_tiles, 1)

    units = [(ch, mat) for ch in range(s.col_parts) for mat in (0, 1)]
    units += [(ch, mat) for ch in range(s.col_parts) for mat in (2, 3)]

    def compute(unit):
        ch, mat = unit
        if mat == 0:
            fill_halos(ch)
            if ch < s.col_parts - 1:
                start_halos(ch + 1)
            if ch == 0:
                start_fluid()
        if mat < 2:
            image_struct(ch, mat)
            project(ref["left_s"], ref["image"].at[0], ch, mat)
            return
        if mat == 2:
            if ch == 0:
                transpose_fluid()
                place_own(ref["ext"], fluid, total_f, TILE)
                fill_fluid()
            image_fluid(ch)
        project(ref["left_f"].at[mat - 2], ref["image"].at[mat - 2], ch, mat)

    def reduce_stage(unit, stage):
        ch, mat = unit
        for rh in range(s.row_parts):
            absorb(ch * s.row_parts + rh, mat, stage)

    count = len(units)
    for turn in range(count + stages - 1):
        if turn < count:
            compute(units[turn])
        for stage in range(stages):
            if 0 <= turn - stage < count:
                reduce_stage(units[turn - stage], stage)
        if turn == 2:
            couple()
        if count // 2 + 1 <= turn < count // 2 + 1 + s.col_bits:
            for part in range(s.parts):
                c_absorb(part, turn - count // 2 - 1)

    for ch in range(s.col_parts):
        for side, sends in ((0, has_next), (1, has_prev)):

            @pl.when(sends)
            def _(side=side, ch=ch):
                halo_whole(side, ch).wait_send()

    for side, sends in ((0, give_next), (1, give_prev)):

        @pl.when(sends)
        def _(side=side):
            for piece in fluid_copies(side):
                piece.wait_send()

    wet_all.wait_send()
    for mask in range(1, nr):
        q_copy(mask).wait_send()
    for mask in far:
        w_copy(mask, False).wait_send()
    for mask in [0] + far:
        w_copy(mask, True).wait_send()
    for part in range(s.parts):
        for bit in range(s.col_bits):
            c_whole(part, bit).wait_send()
        for mat in range(MATS):
            for stage in range(stages):
                whole_stage(part, mat, stage).wait_send()


def reduced(s, struct_cols, fluid_cols, *operands):
    buffers, sems = s.scratch()
    smem = pl.BlockSpec(memory_space=pltpu.SMEM)
    vmem = pl.BlockSpec(memory_space=pltpu.VMEM)
    return pl.pallas_call(
        functools.partial(kernel, s),
        out_shape=jax.ShapeDtypeStruct((MATS + 1, s.bm, s.bn), F32),
        in_specs=[smem, smem] + [vmem] * len(operands),
        out_specs=vmem,
        scratch_shapes=[pltpu.VMEM(shape, dtype) for shape, dtype in buffers.values()]
        + [pltpu.SemaphoreType.DMA(shape) for shape in sems.values()],
        compiler_params=pltpu.CompilerParams(
            collective_id=0, has_side_effects=True, vmem_limit_bytes=VMEM_LIMIT
        ),
        name="reduced",
    )(struct_cols, fluid_cols, *operands)


def on_device(
    nr,
    nc,
    struct_basis,
    fluid_basis,
    stiff_tiles,
    mass_tiles,
    fluid_stiff_tiles,
    fluid_mass_tiles,
    struct_cols,
    fluid_cols,
    wet_rows,
    wet_dest,
    coupling,
):
    rows_s, size = struct_basis.shape
    s = Sizes(nr, nc, rows_s, fluid_basis.shape[0], size, wet_dest.shape[0])
    outs = reduced(
        s,
        struct_cols,
        fluid_cols,
        struct_basis,
        fluid_basis,
        stiff_tiles,
        mass_tiles,
        fluid_stiff_tiles,
        fluid_mass_tiles,
        coupling.T,
        wet_rows[None],
        wet_dest.T,
    )
    return tuple(outs[mat] for mat in range(MATS + 1))


def solution(mesh):
    tiled = P(("row", "col"), None, None, None)
    lined = P(("row", "col"), None)
    return jax.shard_map(
        functools.partial(on_device, mesh.shape["row"], mesh.shape["col"]),
        mesh=mesh,
        in_specs=(lined, lined, tiled, tiled, tiled, tiled, lined, lined, P(("row", "col")), lined, lined),
        out_specs=(P("row", "col"),) * 5,
        check_vma=False,
    )
```

```python
import functools
import types

import jax
import jax.numpy as jnp
from jax import lax
from jax.experimental import pallas as pl
from jax.experimental.pallas import tpu as pltpu
from jax.sharding import PartitionSpec as P

TILE = 128
CAP = 2
MATS = 2
WIDE = 256
VMEM_LIMIT = 67043328
MESH = pl.DeviceIdType.MESH
F32, BF16 = jnp.float32, jnp.bfloat16


def halves(value):
    high = value.astype(BF16)
    low = (value - high.astype(F32)).astype(BF16)
    return high, low


def bits_of(size):
    return size.bit_length() - 1


def subset_offsets(bits):
    offsets = [0]
    for bit in bits:
        offsets = [base + extra for extra in (0, 1 << bit) for base in offsets]
    return offsets


def dot(a, b):
    return jnp.dot(a, b, preferred_element_type=F32)


def dot_t(a, b):
    return lax.dot_general(a, b, (((0,), (0,)), ((), ())), preferred_element_type=F32)


class Sizes:
    def __init__(self, nr, nc, rows_s, rows_f, size, wet):
        self.nr, self.nc, self.size = nr, nc, size
        self.rows_s, self.rows_f, self.wet = rows_s, rows_f, wet
        self.shards = nr * nc
        self.bm, self.bn = size // nr, size // nc
        self.col_parts = 2 if self.bn >= 2 * TILE else 1
        self.row_parts = 4
        self.parts = self.col_parts * self.row_parts
        self.hb, self.bw = self.bm // self.row_parts, self.bn // self.col_parts
        self.chunk = nc * self.bw
        self.qw = max(self.bm, TILE)
        self.some = max(1, min(nr, WIDE // wet))
        self.row_bits, self.col_bits = bits_of(nr), bits_of(nc)
        self.stages = self.row_bits + self.col_bits
        self.total_s = rows_s + 2 * TILE
        self.total_f = rows_f + 2 * TILE

    def scratch(self):
        s = self
        chunks = s.col_parts
        buffers = dict(
            acc=((s.parts, MATS, s.nr, s.nc, s.hb, s.bw), F32),
            acc_c=((s.parts, s.nc, s.hb, s.bw), F32),
            halo_s=((2, s.nc, TILE, s.bn), F32),
            acc_s=((2, s.nr, s.nc, 2, s.bm // 2, s.bn), F32),
            halo_f=((2, s.rows_f, s.size), F32),
            ktile_out=((2, 2, TILE, TILE), F32),
            ktile_in=((2, 2, TILE, TILE), F32),
            left_s=((s.size, 3 * s.rows_s), BF16),
            left_f=((2, s.size, 6 * s.rows_f), BF16),
            dense_s=((2, max(s.rows_s, 2 * s.rows_f), 3 * max(s.total_s, s.total_f)), BF16),
            dense_f=((2 * s.rows_f, 3 * s.total_f), BF16),
            ext=((chunks, 3 * max(s.total_s, s.total_f), s.chunk), BF16),
            image=((2, max(3 * s.rows_s, 6 * s.rows_f), s.chunk), BF16),
            p_out=((s.shards, CAP, s.size), F32),
            p_in=((s.shards, CAP, s.size), F32),
            p_all=((s.shards * CAP, WIDE), F32),
            q_out=((s.wet, s.size), F32),
            q_in=((s.nr, s.wet, s.qw), F32),
            q_left=((2, s.qw, s.some * s.wet), BF16),
            w_all=((s.nr, s.wet, s.size), F32),
        )
        half = s.bm // 2
        blocks = [s.shards >> (stage + 1) for stage in range(s.stages)]
        rows = [s.nr >> (stage + 1) for stage in range(s.row_bits)]
        columns = [s.nc >> (bit + 1) for bit in range(s.col_bits)]
        buffers.update(
            landing=[((s.parts, MATS, n, s.hb, s.bw), F32) for n in blocks],
            landing_s=[((2, s.nc, n, 2, half, s.bn), F32) for n in rows],
            landing_z=[((2, n, 2, half, s.bn), F32) for n in columns],
            landing_c=[((s.parts, n, s.hb, s.bw), F32) for n in columns],
        )
        sems = dict(
            send_sem=(s.parts, MATS, s.stages),
            recv_sem=(s.parts, MATS, s.stages),
            c_send=(s.parts, s.col_bits),
            c_recv=(s.parts, s.col_bits),
            s_send=(2, s.nc, s.row_bits),
            s_recv=(2, s.nc, s.row_bits),
            z_send=(2, s.col_bits, s.nc // 2),
            z_recv=(2, s.col_bits, s.nc // 2),
            halo_send=(2, s.nc),
            halo_recv=(2, s.nc),
            f_send=(2, 2),
            f_recv=(2, 2),
            w_send=(s.nr,),
            w_recv=(s.nr,),
            q_send=(s.nr,),
            q_recv=(s.nr,),
            wet_send=(1,),
            wet_recv=(1,),
        )
        return buffers, sems


def kernel(
    s,
    struct_cols,
    fluid_cols,
    struct,
    fluid,
    stiff_tiles,
    mass_tiles,
    fstiff_tiles,
    fmass_tiles,
    coupling_t,
    wet_rows,
    wet_dest,
    outs,
    *refs,
):
    buffers, sems = s.scratch()
    ref = types.SimpleNamespace()
    left = iter(refs)
    for name, shapes in list(buffers.items()) + list(sems.items()):
        many = isinstance(shapes, list)
        setattr(ref, name, [next(left) for _ in shapes] if many else next(left))
    nr, nc, shards, size = s.nr, s.nc, s.shards, s.size
    rows_s, rows_f = s.rows_s, s.rows_f
    bm, bn, hb, bw = s.bm, s.bn, s.hb, s.bw
    total_s, total_f = s.total_s, s.total_f
    stages = s.stages
    acc, acc_c = ref.acc, ref.acc_c
    row, col = lax.axis_index("row"), lax.axis_index("col")
    block = row * nc + col
    following = lax.rem(block + 1, shards)
    previous = lax.rem(block + shards - 1, shards)
    after = (following // nc, lax.rem(following, nc))
    before = (previous // nc, lax.rem(previous, nc))
    my_row = [lax.rem(row // (1 << b), 2) for b in range(s.row_bits)]
    my_col = [lax.rem(col // (1 << b), 2) for b in range(s.col_bits)]
    row_peer = [(row + (1 - 2 * my_row[b]) * (1 << b), col) for b in range(s.row_bits)]
    col_peer = [(row, col + (1 - 2 * my_col[b]) * (1 << b)) for b in range(s.col_bits)]
    has_next, has_prev = block < shards - 1, block > 0

    def flipped(mask):
        return row + sum(((1 - 2 * my_row[b]) * (1 << b) for b in range(s.row_bits) if mask >> b & 1), 0)

    def ahead(where):
        wraps = (lax.rem(where, nc) == nc - 1).astype(jnp.int32)
        return lax.rem(where // nc + wraps, 2) == 1

    give_next = has_next & ahead(block)
    take_next = has_next & jnp.logical_not(ahead(block))
    take_prev = has_prev & ahead(previous)
    give_prev = has_prev & jnp.logical_not(ahead(previous))

    barrier = pltpu.get_barrier_semaphore()

    def device_at(distance):
        other = lax.rem(block + distance, shards)
        return other, (other // nc, lax.rem(other, nc))

    def greet(distance, carry):
        pl.semaphore_signal(barrier, inc=1, device_id=device_at(distance)[1], device_id_type=MESH)
        return carry

    lax.fori_loop(1, shards, greet, 0)

    def remote(source, target, send, recv, device):
        return pltpu.make_async_remote_copy(
            src_ref=source, dst_ref=target, send_sem=send, recv_sem=recv, device_id=device, device_id_type=MESH
        )

    def wide(q):
        return pl.ds(pl.multiple_of(q * WIDE, WIDE), WIDE)

    def halo_copy(side, c):
        start, device = ((rows_s - TILE, after), (0, before))[side]
        return remote(
            struct.at[pl.ds(start, TILE), pl.ds(c * bn, bn)],
            ref.halo_s.at[side, c],
            ref.halo_send.at[side, c],
            ref.halo_recv.at[side, c],
            device,
        )

    def start_halos(c):
        for side, sends in ((0, has_next), (1, has_prev)):

            @pl.when(sends)
            def _(side=side):
                halo_copy(side, c).start()

    def fluid_copies(side):
        device = (after, before)[side]
        pairs = [(fluid, ref.halo_f.at[side]), (ref.ktile_out.at[side], ref.ktile_in.at[side])]
        return [
            remote(source, target, ref.f_send.at[side, k], ref.f_recv.at[side, k], device)
            for k, (source, target) in enumerate(pairs)
        ]

    def start_fluid():
        for side, sends in ((0, give_next), (1, give_prev)):

            @pl.when(sends)
            def _(side=side):
                for piece in fluid_copies(side):
                    piece.start()

    def send_wet(distance, carry):
        other, device = device_at(distance)
        remote(
            ref.p_out.at[other], ref.p_in.at[block], ref.wet_send.at[0], ref.wet_recv.at[0], device
        ).start()
        return carry

    wet_all = remote(
        ref.p_out.at[pl.ds(0, shards - 1)],
        ref.p_in.at[pl.ds(0, shards - 1)],
        ref.wet_send.at[0],
        ref.wet_recv.at[0],
        after,
    )

    far = [mask for mask in range(2, nr, 2)]

    def w_copy(mask, near):
        slot = flipped(mask) if near else row
        device = (flipped(1), col) if near else (flipped(mask), col)
        place = mask + 1 if near else mask
        return remote(
            ref.w_all.at[slot], ref.w_all.at[slot], ref.w_send.at[place], ref.w_recv.at[place], device
        )

    def q_copy(mask):
        peer = flipped(mask)
        start = pl.multiple_of(peer * bm // s.qw * s.qw, s.qw)
        return remote(
            ref.q_out.at[:, pl.ds(start, s.qw)],
            ref.q_in.at[row],
            ref.q_send.at[mask],
            ref.q_recv.at[mask],
            (peer, col),
        )

    def order_of(part, mat):
        rows = [("row", b) for b in range(s.row_bits)]
        cols = [("col", b) for b in range(s.col_bits)]
        if part % 2:
            rows = rows[:1] + rows[1:][::-1]
        return rows + cols

    def exchange(order, stage):
        axis, bit = order[stage]
        mine = {"row": my_row, "col": my_col}
        places = {}
        for name in ("row", "col"):
            fixed = sum((mine[name][b] * (1 << b) for at, b in order[:stage] if at == name), 0)
            rest = subset_offsets(sorted(b for at, b in order[stage + 1 :] if at == name))
            places[name] = [fixed + extra for extra in rest]
        sent, kept = dict(places), dict(places)
        sent[axis] = [index + (1 - mine[axis][bit]) * (1 << bit) for index in places[axis]]
        kept[axis] = [index + mine[axis][bit] * (1 << bit) for index in places[axis]]
        peer = (row_peer if axis == "row" else col_peer)[bit]
        return sent, kept, peer

    def whole_stage(part, mat, stage):
        peer = exchange(order_of(part, mat), stage)[2]
        here = ref.landing[stage].at[part, mat]
        return remote(here, here, ref.send_sem.at[part, mat, stage], ref.recv_sem.at[part, mat, stage], peer)

    def send(part, mat, stage):
        sent, kept, peer = exchange(order_of(part, mat), stage)
        landing = ref.landing[stage]
        width = len(sent["col"])
        for place, r in enumerate(sent["row"]):
            if width == nc:
                pairs = [(acc.at[part, mat, r], landing.at[part, mat, pl.ds(place * nc, nc)])]
            else:
                pairs = [
                    (acc.at[part, mat, r, c], landing.at[part, mat, place * width + at])
                    for at, c in enumerate(sent["col"])
                ]
            for source, target in pairs:
                remote(
                    source, target, ref.send_sem.at[part, mat, stage], ref.recv_sem.at[part, mat, stage], peer
                ).start()

    def write_out(mat, part, total):
        ch, rh = part // s.row_parts, part % s.row_parts
        outs[mat, pl.ds(rh * hb, hb), pl.ds(ch * bw, bw)] = total

    def absorb(part, mat, stage):
        sent, kept, peer = exchange(order_of(part, mat), stage)
        landing = ref.landing[stage]
        whole_stage(part, mat, stage).wait_recv()
        width = len(kept["col"])
        for place, r in enumerate(kept["row"]):
            if width == nc:

                def add(c, carry, place=place, r=r):
                    acc[part, mat, r, c] = acc[part, mat, r, c] + landing[part, mat, place * nc + c]
                    return carry

                lax.fori_loop(0, nc, add, 0)
            else:
                for at, c in enumerate(kept["col"]):
                    total = acc[part, mat, r, c] + landing[part, mat, place * width + at]
                    if stage < stages - 1:
                        acc[part, mat, r, c] = total
                    else:
                        write_out(2 + mat, part, total)
        if stage < stages - 1:
            send(part, mat, stage + 1)

    col_order = [("col", b) for b in range(s.col_bits)]
    rows_order = [("row", b) for b in range(s.row_bits)]
    s_orders = [rows_order, rows_order[:1] + rows_order[1:][::-1]]

    def s_whole(rh, c, stage):
        here = ref.landing_s[stage].at[rh, c]
        peer = exchange(s_orders[rh], stage)[2]
        return remote(here, here, ref.s_send.at[rh, c, stage], ref.s_recv.at[rh, c, stage], peer)

    def s_send(rh, c, stage):
        sent, kept, peer = exchange(s_orders[rh], stage)
        for place, r in enumerate(sent["row"]):
            remote(
                ref.acc_s.at[rh, r, c],
                ref.landing_s[stage].at[rh, c, place],
                ref.s_send.at[rh, c, stage],
                ref.s_recv.at[rh, c, stage],
                peer,
            ).start()

    def s_absorb(rh, c, stage):
        sent, kept, peer = exchange(s_orders[rh], stage)
        s_whole(rh, c, stage).wait_recv()

        def add(mat, carry):
            for place, r in enumerate(kept["row"]):
                ref.acc_s[rh, r, c, mat] += ref.landing_s[stage][rh, c, place, mat]
            return carry

        lax.fori_loop(0, 2, add, 0)
        if stage < s.row_bits - 1:
            s_send(rh, c, stage + 1)

    def z_copies(rh, bit):
        sent, kept, peer = exchange(col_order, bit)
        return [
            remote(
                ref.acc_s.at[rh, row, c],
                ref.landing_z[bit].at[rh, at],
                ref.z_send.at[rh, bit, at],
                ref.z_recv.at[rh, bit, at],
                peer,
            )
            for at, c in enumerate(sent["col"])
        ]

    def z_absorb(rh, bit, at):
        sent, kept, peer = exchange(col_order, bit)
        z_copies(rh, bit)[at].wait_recv()
        half, c = bm // 2, kept["col"][at]
        for mat in range(2):
            total = ref.acc_s[rh, row, c, mat] + ref.landing_z[bit][rh, at, mat]
            if bit < s.col_bits - 1:
                ref.acc_s[rh, row, c, mat] = total
            else:
                outs[mat, pl.ds(rh * half, half), :] = total

    def z_send(rh, bit, at):
        z_copies(rh, bit)[at].start()

    def c_whole(part, bit):
        here = ref.landing_c[bit].at[part]
        return remote(here, here, ref.c_send.at[part, bit], ref.c_recv.at[part, bit], col_peer[bit])

    def c_send(part, bit):
        sent, kept, peer = exchange(col_order, bit)
        for at, c in enumerate(sent["col"]):
            remote(
                acc_c.at[part, c],
                ref.landing_c[bit].at[part, at],
                ref.c_send.at[part, bit],
                ref.c_recv.at[part, bit],
                peer,
            ).start()

    def c_absorb(part, bit):
        sent, kept, peer = exchange(col_order, bit)
        c_whole(part, bit).wait_recv()
        for at, c in enumerate(kept["col"]):
            total = acc_c[part, c] + ref.landing_c[bit][part, at]
            if bit < s.col_bits - 1:
                acc_c[part, c] = total
            else:
                write_out(4, part, total)
        if bit < s.col_bits - 1:
            c_send(part, bit + 1)

    def select_wet():
        places = lax.broadcasted_iota(jnp.int32, (rows_f, s.wet), 0)
        chooser = (places == wet_rows[...]).astype(F32).astype(BF16)
        high, low = halves(fluid[...])
        ref.w_all[row] = dot_t(chooser, high) + dot_t(chooser, low)

    def project_coupling():
        ch_, cl_ = halves(coupling_t[...])
        for q in range(size // WIDE):
            at = pl.ds(q * WIDE, WIDE)
            sh, sl = halves(struct[:, at])
            value = dot(ch_, sh) + dot(ch_, sl) + dot(cl_, sh)
            for shard in range(shards):
                ref.p_out[shard, :, at] = value[shard * CAP : (shard + 1) * CAP]

    def gather_coupling():
        dest = wet_dest[...]
        mine = (lax.broadcasted_iota(jnp.int32, (shards, s.wet), 0) == dest).astype(F32)
        below = lax.broadcasted_iota(jnp.int32, (s.wet, s.wet), 0) < lax.broadcasted_iota(
            jnp.int32, (s.wet, s.wet), 1
        )
        earlier = dot(mine.astype(BF16), below.astype(F32).astype(BF16))
        slot = jnp.sum(earlier * mine, axis=0, keepdims=True)
        target = dest.astype(F32) * CAP + slot
        places = lax.broadcasted_iota(jnp.int32, (shards * CAP, s.wet), 0).astype(F32)
        chooser = (places == target).astype(F32).astype(BF16)
        wet_all.wait_recv()
        for q in range(size // WIDE):
            at = pl.ds(q * WIDE, WIDE)
            for shard in range(shards):
                ref.p_all[pl.ds(shard * CAP, CAP), :] = ref.p_in[shard, :, at]
            high, low = halves(ref.p_all[...])
            ref.q_out[:, at] = dot_t(chooser, high) + dot_t(chooser, low)
        for mask in range(1, nr):
            q_copy(mask).start()
        own = pl.multiple_of(row * bm // s.qw * s.qw, s.qw)
        ref.q_in[row] = ref.q_out[:, pl.ds(own, s.qw)]

    def couple():
        for mask in range(1, nr):
            q_copy(mask).wait_recv()
        for mask in [0] + far:
            w_copy(mask, True).wait_recv()
        some, rank = s.some, s.some * s.wet
        first = pl.multiple_of(lax.rem(row * bm, s.qw), bm)
        per = WIDE // bw
        for group in range(nr // some):
            here = pl.ds(group * some, some)
            high, low = halves(ref.q_in[here].reshape(rank, s.qw).T)
            ref.q_left[0] = high
            ref.q_left[1] = low
            lh, ll = ref.q_left[0, pl.ds(first, bm)], ref.q_left[1, pl.ds(first, bm)]
            for q in range(size // WIDE):
                wh, wl = halves(ref.w_all[here, :, pl.ds(q * WIDE, WIDE)].reshape(rank, WIDE))
                value = dot(lh, wh) + dot(lh, wl) + dot(ll, wh)
                for k in range(per):
                    c, ch = (q * per + k) // s.col_parts, (q * per + k) % s.col_parts
                    for rh in range(s.row_parts):
                        place = ch * s.row_parts + rh, c
                        piece = value[rh * hb : (rh + 1) * hb, k * bw : (k + 1) * bw]
                        acc_c[place] = piece if group == 0 else acc_c[place] + piece
        for part in range(s.parts):
            c_send(part, 0)

    def transpose_struct():
        left = ref.left_s

        def step(k, carry):
            at = pl.ds(pl.multiple_of(k * TILE, TILE), TILE)
            high, low = halves(struct[:, at].T)
            left[at, pl.ds(0, rows_s)] = high
            left[at, pl.ds(rows_s, rows_s)] = high
            left[at, pl.ds(2 * rows_s, rows_s)] = low
            return carry

        lax.fori_loop(0, size // TILE, step, 0)

    def place_left_f(mats, at, first, value):
        high, low = halves(value)
        for mat in mats:
            left = ref.left_f.at[mat]
            left[at, pl.ds(first, rows_f)] = high
            left[at, pl.ds(2 * rows_f + first, rows_f)] = high
            left[at, pl.ds(4 * rows_f + first, rows_f)] = low

    def transpose_fluid():
        def step(k, carry):
            at = pl.ds(pl.multiple_of(k * TILE, TILE), TILE)
            place_left_f((0, 1), at, 0, fluid[:, at].T)
            return carry

        lax.fori_loop(0, size // TILE, step, 0)

    def place_rows(ext, total, start, at, value):
        count = value.shape[0]
        high, low = halves(value)
        ext[pl.ds(start, count), at] = high
        ext[pl.ds(total + start, count), at] = low
        ext[pl.ds(2 * total + start, count), at] = high

    def place_own(ext, own, total, start):
        for ch in range(s.col_parts):
            for c in range(nc):
                place_rows(ext.at[ch], total, start, pl.ds(c * bw, bw), own[:, pl.ds(c * bn + ch * bw, bw)])

    def tile_sum(tiles, cols, i, c):
        tile = jnp.zeros((TILE, TILE), F32)
        for k in range(tiles.shape[1]):
            tile += jnp.where(cols[i, k] == c, tiles[i, k], 0.0)
        return tile

    def place_tile(dense, at, start, total, tile):
        high, low = halves(tile)
        dense[at, pl.ds(start, TILE)] = high
        dense[at, pl.ds(total + start, TILE)] = high
        dense[at, pl.ds(2 * total + start, TILE)] = low

    def dense_struct(tiles, mat):
        for i in range(rows_s // TILE):
            for c in range(total_s // TILE):
                place_tile(
                    ref.dense_s.at[mat], pl.ds(i * TILE, TILE), c * TILE, total_s, tile_sum(tiles, struct_cols, i, c)
                )

    def dense_fluid(tiles, mat):
        for c in range(3):
            tile = tile_sum(tiles, fluid_cols, 0, c)
            place_tile(ref.dense_f, pl.ds(mat * rows_f, TILE), c * TILE, total_f, tile)
            if c == 0:
                ref.ktile_out[1, mat] = tile
            if c == 2:
                ref.ktile_out[0, mat] = tile

    def ext_of(c):
        return c * bn // s.chunk, pl.ds(c * bn % s.chunk, bn)

    def fill_halos(c):
        which, at = ext_of(c)
        for side, comes in ((0, has_prev), (1, has_next)):

            @pl.when(comes)
            def _(side=side):
                halo_copy(side, c).wait_recv()

            @pl.when(jnp.logical_not(comes))
            def _(side=side):
                ref.halo_s[side, c] = jnp.zeros((TILE, bn), F32)

            start = (0, total_s - TILE)[side]
            place_rows(ref.ext.at[which], total_s, start, at, ref.halo_s[side, c])

    def place_struct():
        for c in range(nc):
            which, at = ext_of(c)
            place_rows(ref.ext.at[which], total_s, TILE, at, struct[:, pl.ds(c * bn, bn)])

    def fill_fluid():
        for side, comes in ((0, take_prev), (1, take_next)):

            @pl.when(comes)
            def _(side=side):
                for piece in fluid_copies(side):
                    piece.wait_recv()

            @pl.when(jnp.logical_not(comes))
            def _(side=side):
                ref.halo_f[side] = jnp.zeros((rows_f, size), F32)
                ref.ktile_in[side] = jnp.zeros((2, TILE, TILE), F32)

            start = (0, total_f - TILE)[side]
            for ch in range(s.col_parts):
                for c in range(nc):
                    place_rows(
                        ref.ext.at[ch],
                        total_f,
                        start,
                        pl.ds(c * bw, bw),
                        ref.halo_f[side, :, pl.ds(c * bn + ch * bw, bw)],
                    )
            for mat in range(2):
                place_tile(ref.dense_s.at[0], pl.ds(mat * rows_f, TILE), start, total_f, ref.ktile_in[side, mat].T)
        for mat in range(2):
            place_tile(ref.dense_s.at[0], pl.ds(mat * rows_f, TILE), TILE, total_f, jnp.zeros((TILE, TILE), F32))
        per = WIDE // bw
        for ch in range(s.col_parts):

            def step(q, carry, ch=ch):
                value = dot(ref.dense_s[0, pl.ds(0, 2 * rows_f), pl.ds(0, 3 * total_f)], ref.ext[ch, pl.ds(0, 3 * total_f), wide(q)])
                for k in range(per):
                    at = pl.ds(pl.multiple_of((q * per + k) * bn + ch * bw, bw), bw)
                    for mat in range(2):
                        piece = value[mat * rows_f : (mat + 1) * rows_f, k * bw : (k + 1) * bw]
                        place_left_f((mat,), at, rows_f, piece.T)
                return carry

            lax.fori_loop(0, s.chunk // WIDE, step, 0)

    def struct_unit(c):
        which, at = ext_of(c)
        half = bm // 2

        def step(mat, carry):
            image = ref.image.at[mat]
            dense = ref.dense_s[mat, pl.ds(0, rows_s), pl.ds(0, 3 * total_s)]
            high, low = halves(dot(dense, ref.ext[which, pl.ds(0, 3 * total_s), at]))
            own = pl.ds(0, bn)
            image[pl.ds(0, rows_s), own] = high
            image[pl.ds(rows_s, rows_s), own] = low
            image[pl.ds(2 * rows_s, rows_s), own] = high
            value = dot(ref.left_s[...], image[pl.ds(0, 3 * rows_s), own])
            for r in range(nr):
                for rh in range(2):
                    start = r * bm + rh * half
                    ref.acc_s[rh, r, c, mat] = value[start : start + half]
            for rh in range(2):
                sent, kept, peer = exchange(s_orders[rh], 0)
                for place, r in enumerate(sent["row"]):
                    remote(
                        ref.acc_s.at[rh, r, c, mat],
                        ref.landing_s[0].at[rh, c, place, mat],
                        ref.s_send.at[rh, c, 0],
                        ref.s_recv.at[rh, c, 0],
                        peer,
                    ).start()
            return carry

        lax.fori_loop(0, 2, step, 0)

    def image_fluid(ch):
        def step(q, carry):
            at = wide(q)
            high, low = halves(dot(ref.dense_f[...], ref.ext[ch, pl.ds(0, 3 * total_f), at]))
            own = [ref.ext[ch, pl.ds(third * total_f + TILE, rows_f), at] for third in range(2)]
            for mat in range(2):
                image = ref.image.at[mat]
                here = slice(mat * rows_f, (mat + 1) * rows_f)
                for third, (value, mine) in enumerate(((high, own[0]), (low, own[1]), (high, own[0]))):
                    image[pl.ds(2 * third * rows_f, rows_f), at] = value[here]
                    image[pl.ds((2 * third + 1) * rows_f, rows_f), at] = mine
            return carry

        lax.fori_loop(0, s.chunk // WIDE, step, 0)

    def project(left, image, ch, mat):
        per = WIDE // bw

        def step(q, carry):
            value = dot(left[...], image[pl.ds(0, left.shape[1]), wide(q)])
            for r in range(nr):
                for rh in range(s.row_parts):
                    start = r * bm + rh * hb
                    for k in range(per):
                        acc[ch * s.row_parts + rh, mat, r, q * per + k] = value[
                            start : start + hb, k * bw : (k + 1) * bw
                        ]
            for rh in range(s.row_parts):
                part = ch * s.row_parts + rh
                sent, kept, peer = exchange(order_of(part, mat), 0)
                for place, r in enumerate(sent["row"]):
                    remote(
                        acc.at[part, mat, r, pl.ds(q * per, per)],
                        ref.landing[0].at[part, mat, pl.ds(place * nc + q * per, per)],
                        ref.send_sem.at[part, mat, 0],
                        ref.recv_sem.at[part, mat, 0],
                        peer,
                    ).start()
            return carry

        lax.fori_loop(0, s.chunk // WIDE, step, 0)

    select_wet()
    pl.semaphore_wait(barrier, shards - 1)
    start_halos(0)
    for mask in far:
        w_copy(mask, False).start()
    w_copy(0, True).start()
    project_coupling()
    lax.fori_loop(1, shards, send_wet, 0)
    start_halos(1)
    ref.p_in[block] = ref.p_out[block]
    transpose_struct()
    place_struct()
    dense_struct(stiff_tiles, 0)
    dense_struct(mass_tiles, 1)

    def forward_wet():
        for mask in far:
            w_copy(mask, False).wait_recv()
            w_copy(mask, True).start()

    units = [("s", c) for c in range(nc)] + [("f", ch, mat) for ch in range(s.col_parts) for mat in range(MATS)]

    def compute(unit):
        if unit[0] == "s":
            c = unit[1]
            fill_halos(c)
            if c + 2 < nc:
                start_halos(c + 2)
            if c == 1:
                start_fluid()
            struct_unit(c)
            return
        ch, mat = unit[1:]
        if mat == 0:
            if ch == 0:
                place_own(ref.ext, fluid, total_f, TILE)
                fill_fluid()
            image_fluid(ch)
        project(ref.left_f.at[mat], ref.image.at[mat], ch, mat)

    def reduce_stage(unit, stage, group=0):
        if unit[0] == "s":
            if stage < s.row_bits:
                for rh in range(2):
                    s_absorb(rh, unit[1], stage)
            return
        ch, mat = unit[1:]
        for rh in (2 * group, 2 * group + 1):
            absorb(ch * s.row_parts + rh, mat, stage)

    count = len(units)
    done = nc - 1 + s.row_bits - 1
    plan = []
    for at, unit in enumerate(units):
        plan.append((at, 0, functools.partial(compute, unit)))
        for stage in range(s.row_bits if unit[0] == "s" else stages):
            late = 0
            for group in range(1 if unit[0] == "s" else s.row_parts // 2):
                turn = at + stage + late + group * 0.5
                plan.append((turn, 1 + stage, functools.partial(reduce_stage, unit, stage, group)))
    plan.append((0, 90, gather_coupling))
    plan.append((0, 91, functools.partial(dense_fluid, fstiff_tiles, 0)))
    plan.append((0, 92, functools.partial(dense_fluid, fmass_tiles, 1)))
    plan.append((1, 90, forward_wet))
    plan.append((2, 90, transpose_fluid))
    plan.append((3, 90, couple))
    for bit in range(s.col_bits):
        for part in range(s.parts):
            plan.append((5 + 2 * bit, 91, functools.partial(c_absorb, part, bit)))
        for rh in range(2):
            for at in range(nc >> (bit + 1)):
                late = nc - 2 - 2 * at if bit == 0 else 0
                plan.append((done + 2 * bit - late, 93, functools.partial(z_send, rh, bit, at)))
                plan.append((done + 2 + 2 * bit - late, 92, functools.partial(z_absorb, rh, bit, at)))
    for at in sorted(range(len(plan)), key=lambda k: plan[k][:2]):
        plan[at][2]()

    for c in range(nc):
        for side, sends in ((0, has_next), (1, has_prev)):

            @pl.when(sends)
            def _(side=side, c=c):
                halo_copy(side, c).wait_send()

    for side, sends in ((0, give_next), (1, give_prev)):

        @pl.when(sends)
        def _(side=side):
            for piece in fluid_copies(side):
                piece.wait_send()

    wet_all.wait_send()
    for mask in range(1, nr):
        q_copy(mask).wait_send()
    for mask in far:
        w_copy(mask, False).wait_send()
    for mask in [0] + far:
        w_copy(mask, True).wait_send()
    for part in range(s.parts):
        for bit in range(s.col_bits):
            c_whole(part, bit).wait_send()
        for mat in range(MATS):
            for stage in range(stages):
                whole_stage(part, mat, stage).wait_send()
    for rh in range(2):
        for c in range(nc):
            for stage in range(s.row_bits):
                s_whole(rh, c, stage).wait_send()
        for bit in range(s.col_bits):
            for copy in z_copies(rh, bit):
                copy.wait_send()


def reduced(s, struct_cols, fluid_cols, *operands):
    buffers, sems = s.scratch()
    smem = pl.BlockSpec(memory_space=pltpu.SMEM)
    vmem = pl.BlockSpec(memory_space=pltpu.VMEM)
    return pl.pallas_call(
        functools.partial(kernel, s),
        out_shape=jax.ShapeDtypeStruct((5, s.bm, s.bn), F32),
        in_specs=[smem, smem] + [vmem] * len(operands),
        out_specs=vmem,
        scratch_shapes=[
            pltpu.VMEM(*pair) for entry in buffers.values() for pair in (entry if isinstance(entry, list) else [entry])
        ]
        + [pltpu.SemaphoreType.DMA(shape) for shape in sems.values()],
        compiler_params=pltpu.CompilerParams(
            collective_id=0, has_side_effects=True, vmem_limit_bytes=VMEM_LIMIT
        ),
        name="reduced",
    )(struct_cols, fluid_cols, *operands)


def on_device(
    nr,
    nc,
    struct_basis,
    fluid_basis,
    stiff_tiles,
    mass_tiles,
    fluid_stiff_tiles,
    fluid_mass_tiles,
    struct_cols,
    fluid_cols,
    wet_rows,
    wet_dest,
    coupling,
):
    rows_s, size = struct_basis.shape
    s = Sizes(nr, nc, rows_s, fluid_basis.shape[0], size, wet_dest.shape[0])
    outs = reduced(
        s,
        struct_cols,
        fluid_cols,
        struct_basis,
        fluid_basis,
        stiff_tiles,
        mass_tiles,
        fluid_stiff_tiles,
        fluid_mass_tiles,
        coupling.T,
        wet_rows[None],
        wet_dest.T,
    )
    return tuple(outs[mat] for mat in range(5))


def solution(mesh):
    tiled = P(("row", "col"), None, None, None)
    lined = P(("row", "col"), None)
    return jax.shard_map(
        functools.partial(on_device, mesh.shape["row"], mesh.shape["col"]),
        mesh=mesh,
        in_specs=(lined, lined, tiled, tiled, tiled, tiled, lined, lined, P(("row", "col")), lined, lined),
        out_specs=(P("row", "col"),) * 5,
        check_vma=False,
    )
```

```python
import functools
import types

import jax
import jax.numpy as jnp
from jax import lax
from jax.experimental import pallas as pl
from jax.experimental.pallas import tpu as pltpu
from jax.sharding import PartitionSpec as P

TILE = 128
CAP = 2
MATS = 2
WIDE = 256
VMEM_LIMIT = 67043328
MESH = pl.DeviceIdType.MESH
F32, BF16 = jnp.float32, jnp.bfloat16


def halves(value):
    high = value.astype(BF16)
    low = (value - high.astype(F32)).astype(BF16)
    return high, low


def bits_of(size):
    return size.bit_length() - 1


def subset_offsets(bits):
    offsets = [0]
    for bit in bits:
        offsets = [base + extra for extra in (0, 1 << bit) for base in offsets]
    return offsets


def dot(a, b):
    return jnp.dot(a, b, preferred_element_type=F32)


def dot_t(a, b):
    return lax.dot_general(a, b, (((0,), (0,)), ((), ())), preferred_element_type=F32)


class Sizes:
    def __init__(self, nr, nc, rows_s, rows_f, size, wet):
        self.nr, self.nc, self.size = nr, nc, size
        self.rows_s, self.rows_f, self.wet = rows_s, rows_f, wet
        self.shards = nr * nc
        self.bm, self.bn = size // nr, size // nc
        self.col_parts = 2 if self.bn >= 2 * TILE else 1
        self.row_parts = 4
        self.parts = self.col_parts * self.row_parts
        self.hb, self.bw = self.bm // self.row_parts, self.bn // self.col_parts
        self.chunk = nc * self.bw
        self.qw = max(self.bm, TILE)
        self.some = max(1, min(nr, WIDE // wet))
        self.row_bits, self.col_bits = bits_of(nr), bits_of(nc)
        self.stages = self.row_bits + self.col_bits
        self.total_s = rows_s + 2 * TILE
        self.total_f = rows_f + 2 * TILE

    def scratch(self):
        s = self
        chunks = s.col_parts
        buffers = dict(
            acc=((s.parts, MATS, s.nr, s.nc, s.hb, s.bw), F32),
            acc_c=((s.parts, s.nc, s.hb, s.bw), F32),
            halo_s=((2, s.nc, TILE, s.bn), F32),
            acc_s=((2, s.nr, s.nc, 2, s.bm // 2, s.bn), F32),
            halo_f=((2, s.rows_f, s.size), F32),
            ktile_out=((2, 2, TILE, TILE), F32),
            ktile_in=((2, 2, TILE, TILE), F32),
            left_s=((s.size, 3 * s.rows_s), BF16),
            left_f=((2, s.size, 6 * s.rows_f), BF16),
            dense_s=((2, max(s.rows_s, 2 * s.rows_f), 3 * max(s.total_s, s.total_f)), BF16),
            dense_f=((2 * s.rows_f, 3 * s.total_f), BF16),
            ext=((chunks, 3 * max(s.total_s, s.total_f), s.chunk), BF16),
            image=((2, max(3 * s.rows_s, 6 * s.rows_f), s.chunk), BF16),
            p_out=((s.shards, CAP, s.size), F32),
            p_in=((s.shards, CAP, s.size), F32),
            p_all=((s.shards * CAP, WIDE), F32),
            q_out=((s.wet, s.size), F32),
            q_in=((s.nr, s.wet, s.qw), F32),
            q_left=((2, s.qw, s.some * s.wet), BF16),
            w_all=((s.nr, s.wet, s.size), F32),
        )
        half = s.bm // 2
        blocks = [s.shards >> (stage + 1) for stage in range(s.stages)]
        rows = [s.nr >> (stage + 1) for stage in range(s.row_bits)]
        columns = [s.nc >> (bit + 1) for bit in range(s.col_bits)]
        buffers.update(
            landing=[((s.parts, MATS, n, s.hb, s.bw), F32) for n in blocks],
            landing_s=[((2, s.nc, n, 2, half, s.bn), F32) for n in rows],
            landing_z=[((2, n, 2, half, s.bn), F32) for n in columns],
            landing_c=[((s.parts, n, s.hb, s.bw), F32) for n in columns],
        )
        sems = dict(
            send_sem=(s.parts, MATS, s.stages),
            recv_sem=(s.parts, MATS, s.stages),
            c_send=(s.parts, s.col_bits),
            c_recv=(s.parts, s.col_bits),
            s_send=(2, s.nc, s.row_bits),
            s_recv=(2, s.nc, s.row_bits),
            z_send=(2, s.col_bits, s.nc // 2),
            z_recv=(2, s.col_bits, s.nc // 2),
            halo_send=(2, s.nc),
            halo_recv=(2, s.nc),
            f_send=(2, 2),
            f_recv=(2, 2),
            w_send=(s.nr,),
            w_recv=(s.nr,),
            q_send=(s.nr,),
            q_recv=(s.nr,),
            wet_send=(1,),
            wet_recv=(1,),
        )
        return buffers, sems


def kernel(
    s,
    struct_cols,
    fluid_cols,
    struct,
    fluid,
    stiff_tiles,
    mass_tiles,
    fstiff_tiles,
    fmass_tiles,
    coupling_t,
    wet_rows,
    wet_dest,
    outs,
    *refs,
):
    buffers, sems = s.scratch()
    ref = types.SimpleNamespace()
    left = iter(refs)
    for name, shapes in list(buffers.items()) + list(sems.items()):
        many = isinstance(shapes, list)
        setattr(ref, name, [next(left) for _ in shapes] if many else next(left))
    nr, nc, shards, size = s.nr, s.nc, s.shards, s.size
    rows_s, rows_f = s.rows_s, s.rows_f
    bm, bn, hb, bw = s.bm, s.bn, s.hb, s.bw
    total_s, total_f = s.total_s, s.total_f
    stages = s.stages
    acc, acc_c = ref.acc, ref.acc_c
    row, col = lax.axis_index("row"), lax.axis_index("col")
    block = row * nc + col
    following = lax.rem(block + 1, shards)
    previous = lax.rem(block + shards - 1, shards)
    after = (following // nc, lax.rem(following, nc))
    before = (previous // nc, lax.rem(previous, nc))
    my_row = [lax.rem(row // (1 << b), 2) for b in range(s.row_bits)]
    my_col = [lax.rem(col // (1 << b), 2) for b in range(s.col_bits)]
    row_peer = [(row + (1 - 2 * my_row[b]) * (1 << b), col) for b in range(s.row_bits)]
    col_peer = [(row, col + (1 - 2 * my_col[b]) * (1 << b)) for b in range(s.col_bits)]
    has_next, has_prev = block < shards - 1, block > 0

    def flipped(mask):
        return row + sum(((1 - 2 * my_row[b]) * (1 << b) for b in range(s.row_bits) if mask >> b & 1), 0)

    def ahead(where):
        wraps = (lax.rem(where, nc) == nc - 1).astype(jnp.int32)
        return lax.rem(where // nc + wraps, 2) == 1

    give_next = has_next & ahead(block)
    take_next = has_next & jnp.logical_not(ahead(block))
    take_prev = has_prev & ahead(previous)
    give_prev = has_prev & jnp.logical_not(ahead(previous))

    barrier = pltpu.get_barrier_semaphore()

    def device_at(distance):
        other = lax.rem(block + distance, shards)
        return other, (other // nc, lax.rem(other, nc))

    def greet(distance, carry):
        pl.semaphore_signal(barrier, inc=1, device_id=device_at(distance)[1], device_id_type=MESH)
        return carry

    lax.fori_loop(1, shards, greet, 0)

    def remote(source, target, send, recv, device):
        return pltpu.make_async_remote_copy(
            src_ref=source, dst_ref=target, send_sem=send, recv_sem=recv, device_id=device, device_id_type=MESH
        )

    def wide(q):
        return pl.ds(pl.multiple_of(q * WIDE, WIDE), WIDE)

    def halo_copy(side, c):
        start, device = ((rows_s - TILE, after), (0, before))[side]
        return remote(
            struct.at[pl.ds(start, TILE), pl.ds(c * bn, bn)],
            ref.halo_s.at[side, c],
            ref.halo_send.at[side, c],
            ref.halo_recv.at[side, c],
            device,
        )

    def start_halos(c):
        for side, sends in ((0, has_next), (1, has_prev)):

            @pl.when(sends)
            def _(side=side):
                halo_copy(side, c).start()

    def fluid_copies(side):
        device = (after, before)[side]
        pairs = [(fluid, ref.halo_f.at[side]), (ref.ktile_out.at[side], ref.ktile_in.at[side])]
        return [
            remote(source, target, ref.f_send.at[side, k], ref.f_recv.at[side, k], device)
            for k, (source, target) in enumerate(pairs)
        ]

    def start_fluid():
        for side, sends in ((0, give_next), (1, give_prev)):

            @pl.when(sends)
            def _(side=side):
                for piece in fluid_copies(side):
                    piece.start()

    def send_wet(distance, carry):
        other, device = device_at(distance)
        remote(
            ref.p_out.at[other], ref.p_in.at[block], ref.wet_send.at[0], ref.wet_recv.at[0], device
        ).start()
        return carry

    wet_all = remote(
        ref.p_out.at[pl.ds(0, shards - 1)],
        ref.p_in.at[pl.ds(0, shards - 1)],
        ref.wet_send.at[0],
        ref.wet_recv.at[0],
        after,
    )

    far = [mask for mask in range(2, nr, 2)]

    def w_copy(mask, near):
        slot = flipped(mask) if near else row
        device = (flipped(1), col) if near else (flipped(mask), col)
        place = mask + 1 if near else mask
        return remote(
            ref.w_all.at[slot], ref.w_all.at[slot], ref.w_send.at[place], ref.w_recv.at[place], device
        )

    def q_copy(mask):
        peer = flipped(mask)
        start = pl.multiple_of(peer * bm // s.qw * s.qw, s.qw)
        return remote(
            ref.q_out.at[:, pl.ds(start, s.qw)],
            ref.q_in.at[row],
            ref.q_send.at[mask],
            ref.q_recv.at[mask],
            (peer, col),
        )

    def order_of(part, mat):
        rows = [("row", b) for b in range(s.row_bits)]
        cols = [("col", b) for b in range(s.col_bits)]
        if part % 2:
            rows = rows[:1] + rows[1:][::-1]
        return rows + cols

    def exchange(order, stage):
        axis, bit = order[stage]
        mine = {"row": my_row, "col": my_col}
        places = {}
        for name in ("row", "col"):
            fixed = sum((mine[name][b] * (1 << b) for at, b in order[:stage] if at == name), 0)
            rest = subset_offsets(sorted(b for at, b in order[stage + 1 :] if at == name))
            places[name] = [fixed + extra for extra in rest]
        sent, kept = dict(places), dict(places)
        sent[axis] = [index + (1 - mine[axis][bit]) * (1 << bit) for index in places[axis]]
        kept[axis] = [index + mine[axis][bit] * (1 << bit) for index in places[axis]]
        peer = (row_peer if axis == "row" else col_peer)[bit]
        return sent, kept, peer

    def whole_stage(part, mat, stage):
        peer = exchange(order_of(part, mat), stage)[2]
        here = ref.landing[stage].at[part, mat]
        return remote(here, here, ref.send_sem.at[part, mat, stage], ref.recv_sem.at[part, mat, stage], peer)

    def send(part, mat, stage):
        sent, kept, peer = exchange(order_of(part, mat), stage)
        landing = ref.landing[stage]
        width = len(sent["col"])
        for place, r in enumerate(sent["row"]):
            if width == nc:
                pairs = [(acc.at[part, mat, r], landing.at[part, mat, pl.ds(place * nc, nc)])]
            else:
                pairs = [
                    (acc.at[part, mat, r, c], landing.at[part, mat, place * width + at])
                    for at, c in enumerate(sent["col"])
                ]
            for source, target in pairs:
                remote(
                    source, target, ref.send_sem.at[part, mat, stage], ref.recv_sem.at[part, mat, stage], peer
                ).start()

    def write_out(mat, part, total):
        ch, rh = part // s.row_parts, part % s.row_parts
        outs[mat, pl.ds(rh * hb, hb), pl.ds(ch * bw, bw)] = total

    def absorb(part, mat, stage):
        sent, kept, peer = exchange(order_of(part, mat), stage)
        landing = ref.landing[stage]
        whole_stage(part, mat, stage).wait_recv()
        width = len(kept["col"])
        for place, r in enumerate(kept["row"]):
            if width == nc:

                def add(c, carry, place=place, r=r):
                    acc[part, mat, r, c] = acc[part, mat, r, c] + landing[part, mat, place * nc + c]
                    return carry

                lax.fori_loop(0, nc, add, 0)
            else:
                for at, c in enumerate(kept["col"]):
                    total = acc[part, mat, r, c] + landing[part, mat, place * width + at]
                    if stage < stages - 1:
                        acc[part, mat, r, c] = total
                    else:
                        write_out(2 + mat, part, total)
        if stage < stages - 1:
            send(part, mat, stage + 1)

    col_order = [("col", b) for b in range(s.col_bits)]
    rows_order = [("row", b) for b in range(s.row_bits)]
    s_orders = [rows_order, rows_order[:1] + rows_order[1:][::-1]]

    def s_whole(rh, c, stage):
        here = ref.landing_s[stage].at[rh, c]
        peer = exchange(s_orders[rh], stage)[2]
        return remote(here, here, ref.s_send.at[rh, c, stage], ref.s_recv.at[rh, c, stage], peer)

    def s_send(rh, c, stage):
        sent, kept, peer = exchange(s_orders[rh], stage)
        for place, r in enumerate(sent["row"]):
            remote(
                ref.acc_s.at[rh, r, c],
                ref.landing_s[stage].at[rh, c, place],
                ref.s_send.at[rh, c, stage],
                ref.s_recv.at[rh, c, stage],
                peer,
            ).start()

    def s_absorb(rh, c, stage):
        sent, kept, peer = exchange(s_orders[rh], stage)
        s_whole(rh, c, stage).wait_recv()

        def add(mat, carry):
            for place, r in enumerate(kept["row"]):
                ref.acc_s[rh, r, c, mat] += ref.landing_s[stage][rh, c, place, mat]
            return carry

        lax.fori_loop(0, 2, add, 0)
        if stage < s.row_bits - 1:
            s_send(rh, c, stage + 1)

    def z_copies(rh, bit):
        sent, kept, peer = exchange(col_order, bit)
        return [
            remote(
                ref.acc_s.at[rh, row, c],
                ref.landing_z[bit].at[rh, at],
                ref.z_send.at[rh, bit, at],
                ref.z_recv.at[rh, bit, at],
                peer,
            )
            for at, c in enumerate(sent["col"])
        ]

    def z_absorb(rh, bit, at):
        sent, kept, peer = exchange(col_order, bit)
        z_copies(rh, bit)[at].wait_recv()
        half, c = bm // 2, kept["col"][at]
        for mat in range(2):
            total = ref.acc_s[rh, row, c, mat] + ref.landing_z[bit][rh, at, mat]
            if bit < s.col_bits - 1:
                ref.acc_s[rh, row, c, mat] = total
            else:
                outs[mat, pl.ds(rh * half, half), :] = total

    def z_send(rh, bit, at):
        z_copies(rh, bit)[at].start()

    def c_whole(part, bit):
        here = ref.landing_c[bit].at[part]
        return remote(here, here, ref.c_send.at[part, bit], ref.c_recv.at[part, bit], col_peer[bit])

    def c_send(part, bit):
        sent, kept, peer = exchange(col_order, bit)
        for at, c in enumerate(sent["col"]):
            remote(
                acc_c.at[part, c],
                ref.landing_c[bit].at[part, at],
                ref.c_send.at[part, bit],
                ref.c_recv.at[part, bit],
                peer,
            ).start()

    def c_absorb(part, bit):
        sent, kept, peer = exchange(col_order, bit)
        c_whole(part, bit).wait_recv()
        for at, c in enumerate(kept["col"]):
            total = acc_c[part, c] + ref.landing_c[bit][part, at]
            if bit < s.col_bits - 1:
                acc_c[part, c] = total
            else:
                write_out(4, part, total)
        if bit < s.col_bits - 1:
            c_send(part, bit + 1)

    def select_wet():
        places = lax.broadcasted_iota(jnp.int32, (rows_f, s.wet), 0)
        chooser = (places == wet_rows[...]).astype(F32).astype(BF16)
        high, low = halves(fluid[...])
        ref.w_all[row] = dot_t(chooser, high) + dot_t(chooser, low)

    def project_coupling():
        ch_, cl_ = halves(coupling_t[...])
        for q in range(size // WIDE):
            at = pl.ds(q * WIDE, WIDE)
            sh, sl = halves(struct[:, at])
            value = dot(ch_, sh) + dot(ch_, sl) + dot(cl_, sh)
            for shard in range(shards):
                ref.p_out[shard, :, at] = value[shard * CAP : (shard + 1) * CAP]

    def gather_coupling():
        dest = wet_dest[...]
        mine = (lax.broadcasted_iota(jnp.int32, (shards, s.wet), 0) == dest).astype(F32)
        below = lax.broadcasted_iota(jnp.int32, (s.wet, s.wet), 0) < lax.broadcasted_iota(
            jnp.int32, (s.wet, s.wet), 1
        )
        earlier = dot(mine.astype(BF16), below.astype(F32).astype(BF16))
        slot = jnp.sum(earlier * mine, axis=0, keepdims=True)
        target = dest.astype(F32) * CAP + slot
        places = lax.broadcasted_iota(jnp.int32, (shards * CAP, s.wet), 0).astype(F32)
        chooser = (places == target).astype(F32).astype(BF16)
        wet_all.wait_recv()
        for q in range(size // WIDE):
            at = pl.ds(q * WIDE, WIDE)
            for shard in range(shards):
                ref.p_all[pl.ds(shard * CAP, CAP), :] = ref.p_in[shard, :, at]
            high, low = halves(ref.p_all[...])
            ref.q_out[:, at] = dot_t(chooser, high) + dot_t(chooser, low)
        for mask in range(1, nr):
            q_copy(mask).start()
        own = pl.multiple_of(row * bm // s.qw * s.qw, s.qw)
        ref.q_in[row] = ref.q_out[:, pl.ds(own, s.qw)]

    def couple():
        for mask in range(1, nr):
            q_copy(mask).wait_recv()
        for mask in [0] + far:
            w_copy(mask, True).wait_recv()
        some, rank = s.some, s.some * s.wet
        first = pl.multiple_of(lax.rem(row * bm, s.qw), bm)
        per = WIDE // bw
        for group in range(nr // some):
            here = pl.ds(group * some, some)
            high, low = halves(ref.q_in[here].reshape(rank, s.qw).T)
            ref.q_left[0] = high
            ref.q_left[1] = low
            lh, ll = ref.q_left[0, pl.ds(first, bm)], ref.q_left[1, pl.ds(first, bm)]
            for q in range(size // WIDE):
                wh, wl = halves(ref.w_all[here, :, pl.ds(q * WIDE, WIDE)].reshape(rank, WIDE))
                value = dot(lh, wh) + dot(lh, wl) + dot(ll, wh)
                for k in range(per):
                    c, ch = (q * per + k) // s.col_parts, (q * per + k) % s.col_parts
                    for rh in range(s.row_parts):
                        place = ch * s.row_parts + rh, c
                        piece = value[rh * hb : (rh + 1) * hb, k * bw : (k + 1) * bw]
                        acc_c[place] = piece if group == 0 else acc_c[place] + piece
        for part in range(s.parts):
            c_send(part, 0)

    def transpose_struct():
        left = ref.left_s

        def step(k, carry):
            at = pl.ds(pl.multiple_of(k * TILE, TILE), TILE)
            high, low = halves(struct[:, at].T)
            left[at, pl.ds(0, rows_s)] = high
            left[at, pl.ds(rows_s, rows_s)] = high
            left[at, pl.ds(2 * rows_s, rows_s)] = low
            return carry

        lax.fori_loop(0, size // TILE, step, 0)

    def place_left_f(mats, at, first, value):
        high, low = halves(value)
        for mat in mats:
            left = ref.left_f.at[mat]
            left[at, pl.ds(first, rows_f)] = high
            left[at, pl.ds(2 * rows_f + first, rows_f)] = high
            left[at, pl.ds(4 * rows_f + first, rows_f)] = low

    def transpose_fluid():
        def step(k, carry):
            at = pl.ds(pl.multiple_of(k * TILE, TILE), TILE)
            place_left_f((0, 1), at, 0, fluid[:, at].T)
            return carry

        lax.fori_loop(0, size // TILE, step, 0)

    def place_rows(ext, total, start, at, value):
        count = value.shape[0]
        high, low = halves(value)
        ext[pl.ds(start, count), at] = high
        ext[pl.ds(total + start, count), at] = low
        ext[pl.ds(2 * total + start, count), at] = high

    def place_own(ext, own, total, start):
        for ch in range(s.col_parts):
            for c in range(nc):
                place_rows(ext.at[ch], total, start, pl.ds(c * bw, bw), own[:, pl.ds(c * bn + ch * bw, bw)])

    def tile_sum(tiles, cols, i, c):
        tile = jnp.zeros((TILE, TILE), F32)
        for k in range(tiles.shape[1]):
            tile += jnp.where(cols[i, k] == c, tiles[i, k], 0.0)
        return tile

    def place_tile(dense, at, start, total, tile):
        high, low = halves(tile)
        dense[at, pl.ds(start, TILE)] = high
        dense[at, pl.ds(total + start, TILE)] = high
        dense[at, pl.ds(2 * total + start, TILE)] = low

    def dense_struct(tiles, mat):
        for i in range(rows_s // TILE):
            for c in range(total_s // TILE):
                place_tile(
                    ref.dense_s.at[mat], pl.ds(i * TILE, TILE), c * TILE, total_s, tile_sum(tiles, struct_cols, i, c)
                )

    def dense_fluid(tiles, mat):
        for c in range(3):
            tile = tile_sum(tiles, fluid_cols, 0, c)
            place_tile(ref.dense_f, pl.ds(mat * rows_f, TILE), c * TILE, total_f, tile)
            if c == 0:
                ref.ktile_out[1, mat] = tile
            if c == 2:
                ref.ktile_out[0, mat] = tile

    def ext_of(c):
        return c * bn // s.chunk, pl.ds(c * bn % s.chunk, bn)

    def fill_halos(c):
        which, at = ext_of(c)
        for side, comes in ((0, has_prev), (1, has_next)):

            @pl.when(comes)
            def _(side=side):
                halo_copy(side, c).wait_recv()

            @pl.when(jnp.logical_not(comes))
            def _(side=side):
                ref.halo_s[side, c] = jnp.zeros((TILE, bn), F32)

            start = (0, total_s - TILE)[side]
            place_rows(ref.ext.at[which], total_s, start, at, ref.halo_s[side, c])

    def place_struct():
        for c in range(nc):
            which, at = ext_of(c)
            place_rows(ref.ext.at[which], total_s, TILE, at, struct[:, pl.ds(c * bn, bn)])

    def fill_fluid():
        for side, comes in ((0, take_prev), (1, take_next)):

            @pl.when(comes)
            def _(side=side):
                for piece in fluid_copies(side):
                    piece.wait_recv()

            @pl.when(jnp.logical_not(comes))
            def _(side=side):
                ref.halo_f[side] = jnp.zeros((rows_f, size), F32)
                ref.ktile_in[side] = jnp.zeros((2, TILE, TILE), F32)

            start = (0, total_f - TILE)[side]
            for ch in range(s.col_parts):
                for c in range(nc):
                    place_rows(
                        ref.ext.at[ch],
                        total_f,
                        start,
                        pl.ds(c * bw, bw),
                        ref.halo_f[side, :, pl.ds(c * bn + ch * bw, bw)],
                    )
            for mat in range(2):
                place_tile(ref.dense_s.at[0], pl.ds(mat * rows_f, TILE), start, total_f, ref.ktile_in[side, mat].T)
        for mat in range(2):
            place_tile(ref.dense_s.at[0], pl.ds(mat * rows_f, TILE), TILE, total_f, jnp.zeros((TILE, TILE), F32))
        per = WIDE // bw
        for ch in range(s.col_parts):

            def step(q, carry, ch=ch):
                value = dot(ref.dense_s[0, pl.ds(0, 2 * rows_f), pl.ds(0, 3 * total_f)], ref.ext[ch, pl.ds(0, 3 * total_f), wide(q)])
                for k in range(per):
                    at = pl.ds(pl.multiple_of((q * per + k) * bn + ch * bw, bw), bw)
                    for mat in range(2):
                        piece = value[mat * rows_f : (mat + 1) * rows_f, k * bw : (k + 1) * bw]
                        place_left_f((mat,), at, rows_f, piece.T)
                return carry

            lax.fori_loop(0, s.chunk // WIDE, step, 0)

    def struct_unit(c):
        which, at = ext_of(c)
        half = bm // 2

        def step(mat, carry):
            image = ref.image.at[mat]
            dense = ref.dense_s[mat, pl.ds(0, rows_s), pl.ds(0, 3 * total_s)]
            high, low = halves(dot(dense, ref.ext[which, pl.ds(0, 3 * total_s), at]))
            own = pl.ds(0, bn)
            image[pl.ds(0, rows_s), own] = high
            image[pl.ds(rows_s, rows_s), own] = low
            image[pl.ds(2 * rows_s, rows_s), own] = high
            value = dot(ref.left_s[...], image[pl.ds(0, 3 * rows_s), own])
            for r in range(nr):
                for rh in range(2):
                    start = r * bm + rh * half
                    ref.acc_s[rh, r, c, mat] = value[start : start + half]
            for rh in range(2):
                sent, kept, peer = exchange(s_orders[rh], 0)
                for place, r in enumerate(sent["row"]):
                    remote(
                        ref.acc_s.at[rh, r, c, mat],
                        ref.landing_s[0].at[rh, c, place, mat],
                        ref.s_send.at[rh, c, 0],
                        ref.s_recv.at[rh, c, 0],
                        peer,
                    ).start()
            return carry

        lax.fori_loop(0, 2, step, 0)

    def image_fluid(ch):
        def step(q, carry):
            at = wide(q)
            high, low = halves(dot(ref.dense_f[...], ref.ext[ch, pl.ds(0, 3 * total_f), at]))
            own = [ref.ext[ch, pl.ds(third * total_f + TILE, rows_f), at] for third in range(2)]
            for mat in range(2):
                image = ref.image.at[mat]
                here = slice(mat * rows_f, (mat + 1) * rows_f)
                for third, (value, mine) in enumerate(((high, own[0]), (low, own[1]), (high, own[0]))):
                    image[pl.ds(2 * third * rows_f, rows_f), at] = value[here]
                    image[pl.ds((2 * third + 1) * rows_f, rows_f), at] = mine
            return carry

        lax.fori_loop(0, s.chunk // WIDE, step, 0)

    def project(left, image, ch, mat):
        per = WIDE // bw

        def step(q, carry):
            value = dot(left[...], image[pl.ds(0, left.shape[1]), wide(q)])
            for r in range(nr):
                for rh in range(s.row_parts):
                    start = r * bm + rh * hb
                    for k in range(per):
                        acc[ch * s.row_parts + rh, mat, r, q * per + k] = value[
                            start : start + hb, k * bw : (k + 1) * bw
                        ]
            for rh in range(s.row_parts):
                part = ch * s.row_parts + rh
                sent, kept, peer = exchange(order_of(part, mat), 0)
                for place, r in enumerate(sent["row"]):
                    remote(
                        acc.at[part, mat, r, pl.ds(q * per, per)],
                        ref.landing[0].at[part, mat, pl.ds(place * nc + q * per, per)],
                        ref.send_sem.at[part, mat, 0],
                        ref.recv_sem.at[part, mat, 0],
                        peer,
                    ).start()
            return carry

        lax.fori_loop(0, s.chunk // WIDE, step, 0)

    select_wet()
    pl.semaphore_wait(barrier, shards - 1)
    start_halos(0)
    for mask in far:
        w_copy(mask, False).start()
    w_copy(0, True).start()
    project_coupling()
    lax.fori_loop(1, shards, send_wet, 0)
    start_halos(1)
    ref.p_in[block] = ref.p_out[block]
    transpose_struct()
    place_struct()
    dense_struct(stiff_tiles, 0)
    dense_struct(mass_tiles, 1)

    def forward_wet():
        for mask in far:
            w_copy(mask, False).wait_recv()
            w_copy(mask, True).start()

    units = [("s", c) for c in range(nc)] + [("f", ch, mat) for ch in range(s.col_parts) for mat in range(MATS)]

    def compute(unit):
        if unit[0] == "s":
            c = unit[1]
            fill_halos(c)
            if c + 2 < nc:
                start_halos(c + 2)
            if c == 1:
                start_fluid()
            struct_unit(c)
            return
        ch, mat = unit[1:]
        if mat == 0:
            if ch == 0:
                place_own(ref.ext, fluid, total_f, TILE)
                fill_fluid()
            image_fluid(ch)
        project(ref.left_f.at[mat], ref.image.at[mat], ch, mat)

    def reduce_stage(unit, stage, group=0):
        if unit[0] == "s":
            if stage < s.row_bits:
                for rh in range(2):
                    s_absorb(rh, unit[1], stage)
            return
        ch, mat = unit[1:]
        for rh in (2 * group, 2 * group + 1):
            absorb(ch * s.row_parts + rh, mat, stage)

    count = len(units)
    done = nc - 1 + s.row_bits - 1
    plan = []
    for at, unit in enumerate(units):
        plan.append((at, 0, functools.partial(compute, unit)))
        for stage in range(s.row_bits if unit[0] == "s" else stages):
            late = 0
            for group in range(1 if unit[0] == "s" else s.row_parts // 2):
                turn = at + stage + late + group * 0.5
                rank = 1 + stage if stage < s.row_bits else 1.2 + 0.01 * stage
                plan.append((turn, rank, functools.partial(reduce_stage, unit, stage, group)))
    plan.append((0, 90, gather_coupling))
    plan.append((0, 91, functools.partial(dense_fluid, fstiff_tiles, 0)))
    plan.append((0, 92, functools.partial(dense_fluid, fmass_tiles, 1)))
    plan.append((1, 90, forward_wet))
    plan.append((2, 90, transpose_fluid))
    plan.append((3, 90, couple))
    for bit in range(s.col_bits):
        for part in range(s.parts):
            plan.append((5 + 2 * bit, 91, functools.partial(c_absorb, part, bit)))
        for rh in range(2):
            for at in range(nc >> (bit + 1)):
                late = nc - 2 - 2 * at if bit == 0 else 0
                plan.append((done + 2 * bit - late, 93 if bit == 0 else 1.4, functools.partial(z_send, rh, bit, at)))
                plan.append((done + 2 + 2 * bit - late, 1.3, functools.partial(z_absorb, rh, bit, at)))
    for at in sorted(range(len(plan)), key=lambda k: plan[k][:2]):
        plan[at][2]()

    for c in range(nc):
        for side, sends in ((0, has_next), (1, has_prev)):

            @pl.when(sends)
            def _(side=side, c=c):
                halo_copy(side, c).wait_send()

    for side, sends in ((0, give_next), (1, give_prev)):

        @pl.when(sends)
        def _(side=side):
            for piece in fluid_copies(side):
                piece.wait_send()

    wet_all.wait_send()
    for mask in range(1, nr):
        q_copy(mask).wait_send()
    for mask in far:
        w_copy(mask, False).wait_send()
    for mask in [0] + far:
        w_copy(mask, True).wait_send()
    for part in range(s.parts):
        for bit in range(s.col_bits):
            c_whole(part, bit).wait_send()
        for mat in range(MATS):
            for stage in range(stages):
                whole_stage(part, mat, stage).wait_send()
    for rh in range(2):
        for c in range(nc):
            for stage in range(s.row_bits):
                s_whole(rh, c, stage).wait_send()
        for bit in range(s.col_bits):
            for copy in z_copies(rh, bit):
                copy.wait_send()


def reduced(s, struct_cols, fluid_cols, *operands):
    buffers, sems = s.scratch()
    smem = pl.BlockSpec(memory_space=pltpu.SMEM)
    vmem = pl.BlockSpec(memory_space=pltpu.VMEM)
    return pl.pallas_call(
        functools.partial(kernel, s),
        out_shape=jax.ShapeDtypeStruct((5, s.bm, s.bn), F32),
        in_specs=[smem, smem] + [vmem] * len(operands),
        out_specs=vmem,
        scratch_shapes=[
            pltpu.VMEM(*pair) for entry in buffers.values() for pair in (entry if isinstance(entry, list) else [entry])
        ]
        + [pltpu.SemaphoreType.DMA(shape) for shape in sems.values()],
        compiler_params=pltpu.CompilerParams(
            collective_id=0, has_side_effects=True, vmem_limit_bytes=VMEM_LIMIT
        ),
        name="reduced",
    )(struct_cols, fluid_cols, *operands)


def on_device(
    nr,
    nc,
    struct_basis,
    fluid_basis,
    stiff_tiles,
    mass_tiles,
    fluid_stiff_tiles,
    fluid_mass_tiles,
    struct_cols,
    fluid_cols,
    wet_rows,
    wet_dest,
    coupling,
):
    rows_s, size = struct_basis.shape
    s = Sizes(nr, nc, rows_s, fluid_basis.shape[0], size, wet_dest.shape[0])
    outs = reduced(
        s,
        struct_cols,
        fluid_cols,
        struct_basis,
        fluid_basis,
        stiff_tiles,
        mass_tiles,
        fluid_stiff_tiles,
        fluid_mass_tiles,
        coupling.T,
        wet_rows[None],
        wet_dest.T,
    )
    return tuple(outs[mat] for mat in range(5))


def solution(mesh):
    tiled = P(("row", "col"), None, None, None)
    lined = P(("row", "col"), None)
    return jax.shard_map(
        functools.partial(on_device, mesh.shape["row"], mesh.shape["col"]),
        mesh=mesh,
        in_specs=(lined, lined, tiled, tiled, tiled, tiled, lined, lined, P(("row", "col")), lined, lined),
        out_specs=(P("row", "col"),) * 5,
        check_vma=False,
    )
```
